256 devices in a mesh: tm: 32 (over x, y, core), space: 8 (over z).
Axes of the slice: x: 4, y: 4, z: 8, core: 2. Of those that a mesh axis runs over, the one named last changes fastest.
Arguments:
- queries: bfloat16 [32, 64, 80, 2240], P('tm', 'space'), may hold values from -6 to 6
- keys: bfloat16 [32, 64, 80, 2240], P('tm', 'space'), may hold values from -60 to 60
- values: bfloat16 [32, 64, 80, 2240], P('tm', 'space'), may hold values from -6 to 6
- conv_weight: float32 [3, 3, 2240], replicated, may hold values from -5 to 5
- w_out: bfloat16 [2240, 2240], P('tm', 'space'), may hold values from -0.125 to 0.125
Outputs:
- layer_out: bfloat16 [32, 64, 80, 2240], P('tm', 'space')
The draws below stay inside these ranges and needn't reach their ends.
All inputs are finite; a program needn't handle non-finite values.
Results may differ from the reference program's by a relative error of at most 0.001.
The reference program's roundings to bfloat16 on the way (of `mix`) count: a program that leaves them out, or rounds other values in their place, can miss the bound.
Values may be sent and summed in bfloat16 or wider, within the bound.
A program may use at most 128 MiB of HBM per device.

```python
import math
import jax
import jax.numpy as jnp
from jax import lax

HEADS = 20
HEAD_DIM = 112
COLS = 80
D = 2240
ROWS = 64
FRAMES = 32


def token_channels(key):
    pick_key = jax.random.fold_in(key, 5)
    return jax.random.randint(pick_key, (FRAMES, ROWS, COLS, HEADS), 0, HEAD_DIM).astype(jnp.int32)


def draw_keys(key, part):
    chosen = token_channels(key)
    base = jax.random.fold_in(key, 11)
    scale_key, noise_key = jax.random.split(base)
    frame_scale = jnp.exp(jax.random.uniform(scale_key, (FRAMES, 1, 1, 1, 1), jnp.float32, 0.0, math.log(10.0)))
    noise = jnp.clip(jax.random.normal(noise_key, (FRAMES, ROWS, COLS, HEADS, HEAD_DIM), jnp.float32), -3.0, 3.0)
    feature_ids = jnp.arange(HEAD_DIM, dtype=jnp.int32).reshape(1, 1, 1, 1, HEAD_DIM)
    marked = (feature_ids == chosen[..., None]).astype(jnp.float32)
    raw = frame_scale * (0.6 * noise - 1.6 + 4.6 * marked)
    return raw.reshape(FRAMES, ROWS, COLS, D).astype(jnp.bfloat16)


def draw_values(key, part):
    chosen = token_channels(key)
    base = jax.random.fold_in(key, 23)
    table_key, noise_key = jax.random.split(base)
    table = 2.0 * jnp.clip(jax.random.normal(table_key, (FRAMES, HEADS, HEAD_DIM, HEAD_DIM), jnp.float32), -1.5, 1.5)
    noise = 0.5 * jnp.clip(jax.random.normal(noise_key, (FRAMES, ROWS, COLS, HEADS, HEAD_DIM), jnp.float32), -6.0, 6.0)
    frame_ids = jnp.arange(FRAMES, dtype=jnp.int32).reshape(FRAMES, 1, 1, 1)
    head_ids = jnp.arange(HEADS, dtype=jnp.int32).reshape(1, 1, 1, HEADS)
    selected = table[frame_ids, head_ids, chosen]
    raw = jnp.clip(selected + noise, -6.0, 6.0)
    return raw.reshape(FRAMES, ROWS, COLS, D).astype(jnp.bfloat16)


def steps_of(stream_key, dims, cuts, smallest, top_value):
    def one(axis_at, parts):
        heights = jax.random.uniform(jax.random.fold_in(jax.random.fold_in(stream_key, 6), axis_at), (parts,), jnp.float32, smallest / len(cuts), top_value / len(cuts))
        return jnp.repeat(jnp.exp(heights), dims[axis_at] // parts).reshape((-1,) + (1,) * (len(dims) - axis_at - 1))

    factor_of = one(*cuts[0])
    for cut in cuts[1:]:
        factor_of = factor_of * one(*cut)
    return factor_of


def normal_values(rng, dims, spread, most, cuts=(), held_as=jnp.bfloat16):
    factor_of = steps_of(rng, dims, cuts, -0.22, 0.18) if cuts else 1.0
    values = jax.random.normal(rng, dims, jnp.float32) * spread * factor_of
    return jnp.minimum(jnp.maximum(values, -most), most).astype(held_as)


def setup_inputs(seed: int = 0) -> dict:
    splits = jax.random.split(jax.random.key(seed), 6)
    return {
        "queries": normal_values(splits[0], (FRAMES, ROWS, COLS, D), 1.0, 6.0, ((0, 32), (1, 8))),
        "keys": draw_keys(jax.random.fold_in(splits[5], 71), 0),
        "values": draw_values(jax.random.fold_in(splits[5], 71), 0),
        "conv_weight": normal_values(splits[3], (3, 3, D), 0.35, 5.0, (), jnp.float32),
        "w_out": normal_values(splits[4], (D, D), D ** -0.5, 0.125, ((0, 32), (1, 8))),
    }


epsilon = 1e-6


def frame_state(pair):
    key_frame, value_frame = pair
    key_pos = jnp.maximum(key_frame, 0).astype(jnp.float32).reshape(-1, HEADS, HEAD_DIM)
    value_heads = value_frame.astype(jnp.float32).reshape(-1, HEADS, HEAD_DIM)
    return jnp.einsum('the,thf->hef', key_pos, value_heads), jnp.sum(key_pos, axis=0)


def reference(queries, keys, values, conv_weight, w_out):
    states, key_sums = lax.map(frame_state, (keys, values))
    states = jnp.cumsum(states, axis=0)
    key_sums = jnp.cumsum(key_sums, axis=0)

    def frame_out(group):
        query_frame, value_frame, state_now, sum_now = group
        state_low = lax.optimization_barrier(state_now.astype(jnp.bfloat16)).astype(jnp.float32)
        sum_low = lax.optimization_barrier(sum_now.astype(jnp.bfloat16)).astype(jnp.float32)
        query_pos = jnp.maximum(query_frame, 0).astype(jnp.float32).reshape(-1, HEADS, HEAD_DIM)
        numer = jnp.einsum('the,hef->thf', query_pos, state_low)
        denom = jnp.einsum('the,he->th', query_pos, sum_low)
        attn = (numer / (denom[:, :, None] + epsilon)).reshape(ROWS, COLS, D)
        padded = jnp.pad(value_frame.astype(jnp.float32), ((1, 1), (1, 1), (0, 0)))
        conv = jnp.zeros((ROWS, COLS, D), jnp.float32)
        for row_off in range(3):
            for col_off in range(3):
                conv = conv + padded[row_off:row_off + ROWS, col_off:col_off + COLS] * conv_weight[row_off, col_off]
        mix = (attn + conv).astype(jnp.bfloat16).reshape(ROWS * COLS, D)
        result = jnp.dot(mix, w_out, preferred_element_type=jnp.float32)
        return result.astype(jnp.bfloat16).reshape(ROWS, COLS, D)

    return lax.map(frame_out, (queries, values, states, key_sums))
```

```python
import functools

import jax
import jax.numpy as jnp
from jax import lax
from jax.experimental import pallas as pl
from jax.experimental.pallas import tpu as pltpu
from jax.sharding import PartitionSpec as P

HEADS = 20
HD = 112
D = HEADS * HD
ROWS, COLS = 8, 80
TOK = ROWS * COLS
LANES = 128
TILES = 18
DP = TILES * LANES
BLK, BLKP = 70, 72
UNITS = 7
NZ = 8
EPS = 1e-06
MESH = pl.DeviceIdType.MESH
F32, BF16 = jnp.float32, jnp.bfloat16


def feature_of(pos):
    return BLK * (pos // BLKP) + min(pos % BLKP, BLK - 1)


def spread_window(j):
    lo = feature_of(LANES * j) // LANES
    lo = min(lo, TILES - 2)
    return lo, LANES * lo, min(LANES * (lo + 2), D)


def spread_matrix(j, start, stop):
    shape = (stop - start, LANES)
    pos = LANES * j + lax.broadcasted_iota(jnp.int32, shape, 1)
    block = lax.shift_right_logical(pos * 14564, 20)
    inside = pos - BLKP * block
    feature = BLK * block + inside
    row = start + lax.broadcasted_iota(jnp.int32, shape, 0)
    return jnp.where((row == feature) & (inside < BLK), 1.0, 0.0).astype(BF16)


def dot(a, b):
    return jnp.dot(a, b, preferred_element_type=F32)


def add_mod(a, b, n):
    return lax.rem(a + b + 2 * n, n)


def gather_kernel(
    k_hbm, v_hbm, w_hbm, cw_ref, conv_hbm, s_hbm, wg_hbm,
    kn, vn, kt, vp, cwp, conv, z_ref, fwd, bwd, own, scan, pre, xs, back, s_own, wa, wown,
    local_sem, halo_send, halo_recv, wa_send, wa_recv, rs_send, rs_recv, sc_send, sc_recv,
    xs_send, xs_recv, bk_send, bk_recv, ag_send, ag_recv, wg_send, wg_recv,
):
    tm, z = lax.axis_index("tm"), lax.axis_index("space")
    core, y, x = lax.rem(tm, 2), lax.rem(lax.div(tm, 2), 4), lax.div(tm, 8)
    member = lax.rem(tm, 8)
    dr = 1 - 2 * core

    def at(xx, yy, cc):
        return 8 * xx + 2 * yy + cc

    def along_a(k):
        other = add_mod(jnp.where(core == 0, x, y), k, 4)
        return jnp.where(core == 0, at(other, y, core), at(x, other, core))

    def along(ka, kb):
        px = add_mod(x, jnp.where(core == 0, ka, kb), 4)
        py = add_mod(y, jnp.where(core == 0, kb, ka), 4)
        return at(px, py, core)

    partner = at(x, y, 1 - core)
    everything = []

    def remote(src, dst, send, recv, to_tm, to_z):
        return pltpu.make_async_remote_copy(
            src_ref=src, dst_ref=dst, send_sem=send, recv_sem=recv,
            device_id={"tm": to_tm, "space": to_z}, device_id_type=MESH,
        )

    def start(copy):
        copy.start()
        everything.append(copy)
        return copy

    barrier = pltpu.get_barrier_semaphore()
    friends = [(tm, add_mod(z, o, NZ)) for o in range(1, NZ)]
    friends += [(8 * x + add_mod(member, o, 8), z) for o in range(1, 8)]
    friends += [(add_mod(tm, 8 * o, 32), z) for o in range(1, 4)]
    for to_tm, to_z in friends:
        pl.semaphore_signal(barrier, inc=1, device_id={"tm": to_tm, "space": to_z}, device_id_type=MESH)
    loads = [
        pltpu.make_async_copy(k_hbm, kn, local_sem.at[0]),
        pltpu.make_async_copy(v_hbm, vn.at[pl.ds(COLS, TOK)], local_sem.at[1]),
    ]
    for copy in loads:
        copy.start()
    pl.semaphore_wait(barrier, len(friends))

    wa_mine = pltpu.make_async_copy(w_hbm, wa.at[z], local_sem.at[2])
    wa_mine.start()
    for o in range(1, NZ):
        start(remote(w_hbm, wa.at[z], wa_send.at[o - 1], wa_recv.at[o - 1], tm, add_mod(z, o, NZ)))
    halo = [
        remote(v_hbm.at[pl.ds(0, COLS)], vn.at[pl.ds(COLS + TOK, COLS)], halo_send.at[0], halo_recv.at[0], tm, add_mod(z, -1, NZ)),
        remote(v_hbm.at[pl.ds(TOK - COLS, COLS)], vn.at[pl.ds(0, COLS)], halo_send.at[1], halo_recv.at[1], tm, add_mod(z, 1, NZ)),
    ]
    for copy in halo:
        start(copy)

    def partial_state():
        loads[0].wait()
        for i in range(TILES):
            lo, hi = LANES * i, min(LANES * (i + 1), D)
            kt[lo:hi, :] = jnp.maximum(kn[:, lo:hi], 0).T
        loads[1].wait()
        ones = jnp.ones((TOK, LANES), BF16)
        lane = lax.broadcasted_iota(jnp.int32, (HD, LANES), 1)
        sums = jnp.zeros((HD, LANES), F32)
        for j in range(TILES):
            lo, hi = LANES * j, min(LANES * (j + 1), D)
            tile = vn[COLS : COLS + TOK, lo:hi]
            if hi - lo < LANES:
                eye = lax.broadcasted_iota(jnp.int32, (hi - lo, LANES), 0) == lax.broadcasted_iota(jnp.int32, (hi - lo, LANES), 1)
                tile = dot(tile, jnp.where(eye, 1.0, 0.0).astype(BF16)).astype(BF16)
            first, last = lo // HD, (hi - 1) // HD
            g = dot(kt[HD * first : HD * (last + 1), :], jnp.concatenate([tile, ones], axis=1))
            part = g[:HD, :LANES]
            for h in range(first, last + 1):
                rows = g[HD * (h - first) : HD * (h - first + 1)]
                part = jnp.where(lane < HD * h - lo, part, rows[:, :LANES])
                sums = jnp.where(lane == D - LANES * (TILES - 1) + h, rows[:, LANES:], sums)
            if j == TILES - 1:
                part = jnp.where(lane < D - lo, part, sums)
            for r in range(UNITS):
                z_ref[UNITS * j + r] = part[16 * r : 16 * (r + 1)]
        z_ref[UNITS * TILES] = jnp.zeros((16, LANES), F32)
        z_ref[UNITS * TILES + 1] = jnp.zeros((16, LANES), F32)

    def ring(forward, s, u):
        hops = 4 if forward else 3
        way = dr if forward else -dr
        slots = fwd if forward else bwd
        chunk = add_mod(z, way * (hops - s), NZ)
        place = pl.ds(8 * u, 8)
        sem = (0 if forward else 8) + 2 * s + u
        if s == 0:
            src = z_ref.at[pl.ds(16 * chunk + 8 * u, 8)]
        else:
            everything_rs[(forward, s - 1, u)].wait_recv()
            slots[s - 1, place] += z_ref[pl.ds(16 * chunk + 8 * u, 8)]
            src = slots.at[s - 1, place]
        copy = remote(src, slots.at[s, place], rs_send.at[sem], rs_recv.at[sem], tm, add_mod(z, way, NZ))
        copy.start()
        everything_rs[(forward, s, u)] = copy

    everything_rs = {}

    def ring_step(s):
        for u in range(2):
            ring(True, s, u)
            if s < 3:
                ring(False, s, u)

    def ring_end():
        for u in range(2):
            everything_rs[(True, 3, u)].wait_recv()
            everything_rs[(False, 2, u)].wait_recv()
            place = pl.ds(8 * u, 8)
            own[place] = z_ref[pl.ds(16 * z + 8 * u, 8)] + fwd[3, place] + bwd[2, place]

    def scan_send():
        for o in range(1, 8):
            other = add_mod(member, o, 8)
            start(remote(own.at[pl.ds(2 * other, 2)], scan.at[member], sc_send.at[o - 1], sc_recv.at[o - 1], 8 * x + other, z))
        scan[member] = own[pl.ds(2 * member, 2)]

    def scan_group():
        for o in range(1, 8):
            remote(own.at[pl.ds(0, 2)], scan.at[0], sc_send.at[o - 1], sc_recv.at[o - 1], tm, z).wait_recv()
        total = jnp.zeros((2, 16, LANES), F32)
        for m in range(8):
            total = total + scan[m]
            pre[m] = total
        for o in range(1, 4):
            start(remote(pre.at[7], xs.at[x], xs_send.at[o - 1], xs_recv.at[o - 1], add_mod(tm, 8 * o, 32), z))
        xs[x] = total

    def scan_back():
        for o in range(1, 4):
            remote(pre.at[7], xs.at[0], xs_send.at[o - 1], xs_recv.at[o - 1], tm, z).wait_recv()
        before = jnp.zeros((2, 16, LANES), F32)
        for k in range(4):
            before = before + jnp.where(k < x, xs[k], 0.0)
        for m in range(8):
            back[m] = (before + pre[m]).astype(BF16)
        for o in range(1, 8):
            other = add_mod(member, o, 8)
            start(remote(back.at[other], s_own.at[pl.ds(2 * member, 2)], bk_send.at[o - 1], bk_recv.at[o - 1], 8 * x + other, z))
        s_own[pl.ds(2 * member, 2)] = back[member]

    def share_state():
        for o in range(1, 8):
            remote(back.at[0], s_own.at[pl.ds(0, 2)], bk_send.at[o - 1], bk_recv.at[o - 1], tm, z).wait_recv()
        dst = s_hbm.at[pl.ds(16 * z, 16)]
        for o in range(1, NZ):
            start(remote(s_own, dst, ag_send.at[o - 1], ag_recv.at[o - 1], tm, add_mod(z, o, NZ)))
        copy = pltpu.make_async_copy(s_own, dst, local_sem.at[3])
        copy.start()
        return copy

    def rows_of(owner, half=None):
        lo, n = (0, BLKP) if half is None else ((0, 40) if half == 0 else (40, 32))
        return wg_hbm.at[pl.ds(pl.multiple_of(BLKP * owner + lo, 8), n)]

    def w_send(n, src, dst, to_tm):
        start(remote(src, dst, wg_send.at[n], wg_recv.at[n], to_tm, z))

    def w_wait(n, ref):
        remote(ref, ref, wg_send.at[n], wg_recv.at[n], tm, z).wait_recv()

    deltas = (0, -1, 1, 2)

    def w_out_b(g, src=None):
        owner = along(deltas[g], 0)
        ref = rows_of(owner) if src is None else src
        w_send(4 + 4 * g, ref, rows_of(owner), along(0, 1))
        w_send(5 + 4 * g, ref, rows_of(owner), along(0, -1))
        w_send(20 + 4 * g, ref, rows_of(owner), partner)

    def w_assemble():
        wa_mine.wait()
        for o in range(1, NZ):
            remote(w_hbm, wa.at[0], wa_send.at[o - 1], wa_recv.at[o - 1], tm, z).wait_recv()
        wown[...] = jnp.zeros((BLKP, DP), BF16)
        width = D // NZ
        for j in range(TILES):
            lo, hi = LANES * j, min(LANES * (j + 1), D)
            acc = jnp.zeros((BLK, LANES), F32)
            for b in range(lo // width, (hi - 1) // width + 1):
                row = width * b + lax.broadcasted_iota(jnp.int32, (width, LANES), 0)
                col = lo + lax.broadcasted_iota(jnp.int32, (width, LANES), 1)
                acc = acc + dot(wa[b], jnp.where(row == col, 1.0, 0.0).astype(BF16))
            wown[0:BLK, lo : lo + LANES] = acc.astype(BF16)
        mine = pltpu.make_async_copy(wown, rows_of(tm), local_sem.at[4])
        mine.start()
        w_send(0, wown, rows_of(tm), along(1, 0))
        w_send(1, wown, rows_of(tm), along(-1, 0))
        w_out_b(0, wown)
        return mine

    def w_a_full():
        low, high = along(-1, 0), along(1, 0)
        w_wait(0, rows_of(low))
        w_send(2, rows_of(low, 0), rows_of(low, 0), high)
        w_out_b(1)
        w_wait(1, rows_of(high))
        w_send(3, rows_of(high, 1), rows_of(high, 1), low)
        w_out_b(2)

    def w_a_half():
        w_wait(2, rows_of(along(2, 0), 0))
        w_wait(3, rows_of(along(2, 0), 1))
        w_out_b(3)

    def w_b_full(g):
        low, high = along(deltas[g], -1), along(deltas[g], 1)
        w_wait(4 + 4 * g, rows_of(low))
        w_send(6 + 4 * g, rows_of(low, 0), rows_of(low, 0), along(0, 1))
        w_send(21 + 4 * g, rows_of(low), rows_of(low), partner)
        w_wait(5 + 4 * g, rows_of(high))
        w_send(7 + 4 * g, rows_of(high, 1), rows_of(high, 1), along(0, -1))
        w_send(22 + 4 * g, rows_of(high), rows_of(high), partner)

    def w_b_half(g):
        far = along(deltas[g], 2)
        w_wait(6 + 4 * g, rows_of(far, 0))
        w_wait(7 + 4 * g, rows_of(far, 1))
        w_send(23 + 4 * g, rows_of(far), rows_of(far), partner)

    def w_end():
        for n in range(20, 36):
            w_wait(n, rows_of(0))

    def conv_prepare():
        for copy in halo:
            copy.wait_recv()

        @pl.when(z == 0)
        def _():
            vn[0:COLS, :] = jnp.zeros((COLS, D), BF16)

        @pl.when(z == NZ - 1)
        def _():
            vn[COLS + TOK :, :] = jnp.zeros((COLS, D), BF16)

        for j in range(TILES):
            _, lo, hi = spread_window(j)
            spread = spread_matrix(j, lo, hi)
            place = slice(LANES * j, LANES * (j + 1))
            vp[:, place] = dot(vn[:, lo:hi], spread).astype(BF16)
            for a in range(3):
                rest = cw_ref[a, :, lo:hi]
                total = jnp.zeros((3, LANES), F32)
                for _ in range(3):
                    piece = rest.astype(BF16)
                    total = total + dot(piece, spread)
                    rest = rest - piece.astype(F32)
                cwp[a, 0:3, place] = total

    def conv_rows(first, last):
        row = lax.broadcasted_iota(jnp.int32, (COLS, LANES), 0)

        @pl.loop(first, last)
        def _(r):
            base = pl.multiple_of(COLS * r, 16)
            for j in range(TILES):
                place = slice(LANES * j, LANES * (j + 1))
                lines = [vp[pl.ds(base + COLS * a, COLS), place].astype(F32) for a in range(3)]
                sums = []
                for b in range(3):
                    sums.append(sum(lines[a] * cwp[a, b : b + 1, place] for a in range(3)))
                left = jnp.where(row == 0, 0.0, pltpu.roll(sums[0], 1, 0))
                right = jnp.where(row == COLS - 1, 0.0, pltpu.roll(sums[2], COLS - 1, 0))
                conv[pl.ds(base, COLS), place] = sums[1] + left + right

    partial_state()
    ring_step(0)
    mine = w_assemble()
    conv_prepare()
    ring_step(1)
    conv_rows(0, 2)
    ring_step(2)
    w_a_full()
    conv_rows(2, 5)
    ring_step(3)
    w_b_full(0)
    conv_rows(5, 8)
    conv_out = pltpu.make_async_copy(conv, conv_hbm, local_sem.at[5])
    conv_out.start()
    ring_end()
    scan_send()
    w_a_half()
    scan_group()
    mine.wait()
    scan_back()
    w_b_full(1)
    state_mine = share_state()
    w_b_full(2)
    w_b_half(0)
    w_b_full(3)
    w_b_half(1)
    w_b_half(2)
    w_b_half(3)
    for o in range(1, NZ):
        remote(s_own, s_hbm.at[pl.ds(0, 16)], ag_send.at[o - 1], ag_recv.at[o - 1], tm, z).wait_recv()
    w_end()
    for copy in everything + list(everything_rs.values()):
        copy.wait_send()
    state_mine.wait()
    conv_out.wait()


def gather(k, v, w, cw):
    dma = pltpu.SemaphoreType.DMA
    any_space = pl.BlockSpec(memory_space=pl.ANY)
    return pl.pallas_call(
        gather_kernel,
        out_shape=(
            jax.ShapeDtypeStruct((TOK, DP), F32),
            jax.ShapeDtypeStruct((16 * NZ, 16, LANES), BF16),
            jax.ShapeDtypeStruct((32 * BLKP, DP), BF16),
        ),
        in_specs=[any_space, any_space, any_space, pl.BlockSpec(memory_space=pltpu.VMEM)],
        out_specs=(any_space,) * 3,
        scratch_shapes=[
            pltpu.VMEM((TOK, D), BF16),
            pltpu.VMEM((TOK + 2 * COLS, D), BF16),
            pltpu.VMEM((D, TOK), BF16),
            pltpu.VMEM((TOK + 2 * COLS, DP), BF16),
            pltpu.VMEM((3, 8, DP), F32),
            pltpu.VMEM((TOK, DP), F32),
            pltpu.VMEM((16 * NZ, 16, LANES), F32),
            pltpu.VMEM((4, 16, 16, LANES), F32),
            pltpu.VMEM((3, 16, 16, LANES), F32),
            pltpu.VMEM((16, 16, LANES), F32),
            pltpu.VMEM((8, 2, 16, LANES), F32),
            pltpu.VMEM((8, 2, 16, LANES), F32),
            pltpu.VMEM((4, 2, 16, LANES), F32),
            pltpu.VMEM((8, 2, 16, LANES), BF16),
            pltpu.VMEM((16, 16, LANES), BF16),
            pltpu.VMEM((NZ, BLK, D // NZ), BF16),
            pltpu.VMEM((BLKP, DP), BF16),
            dma((6,)), dma((2,)), dma((2,)), dma((7,)), dma((7,)), dma((14,)), dma((14,)),
            dma((7,)), dma((7,)), dma((3,)), dma((3,)), dma((7,)), dma((7,)), dma((7,)), dma((7,)),
            dma((36,)), dma((36,)),
        ],
        compiler_params=pltpu.CompilerParams(
            collective_id=0, has_side_effects=True, vmem_limit_bytes=48 << 20
        ),
        name="state_and_gather",
    )(k, v, w, cw)


def heads_of(j):
    features = [
        feature_of(p) for p in range(LANES * j, LANES * (j + 1)) if p % BLKP < BLK
    ]
    first, last = min(features) // HD, max(features) // HD
    lo = HD * first // LANES * LANES
    hi = min(-(-HD * (last + 1) // LANES) * LANES, D)
    return first, last, lo, hi


def project_kernel(q_hbm, conv_hbm, s_hbm, w_hbm, out_ref, qv, cv, sv, sn, band, mix, wv, sem):
    n = pl.program_id(0)
    steps = DP // 256
    copies = [
        pltpu.make_async_copy(s_hbm, sv, sem.at[0]),
        pltpu.make_async_copy(q_hbm, qv, sem.at[1]),
        pltpu.make_async_copy(conv_hbm, cv, sem.at[2]),
    ]
    weights = [
        pltpu.make_async_copy(
            w_hbm.at[:, pl.ds(256 * t, 256)], wv.at[:, pl.ds(256 * t, 256)], sem.at[3 + t]
        )
        for t in range(steps)
    ]

    @pl.when(n == 0)
    def _():
        for copy in copies + weights:
            copy.start()
        copies[0].wait()
        for j in range(TILES):
            for r in range(UNITS):
                sn[16 * r : 16 * (r + 1), LANES * j : LANES * (j + 1)] = sv[UNITS * j + r]
        sums = sn[:, LANES * (TILES - 1) :]
        base = D - LANES * (TILES - 1)
        for j in range(TILES):
            first, last, lo, hi = heads_of(j)
            band[j] = jnp.zeros(band.shape[1:], BF16)
            _, w_lo, _ = spread_window(j)
            w_hi = w_lo + 2 * LANES
            spread = spread_matrix(j, w_lo, w_hi)
            state = dot(sn[:, w_lo:w_hi], spread).astype(BF16)
            pos = LANES * j + lax.broadcasted_iota(jnp.int32, (LANES, LANES), 1)
            block = lax.shift_right_logical(pos * 14564, 20)
            inside = pos - BLKP * block
            feature = BLK * block + inside
            row = lax.broadcasted_iota(jnp.int32, (LANES, LANES), 0)
            for h in range(first, last + 1):
                member = (inside < BLK) & (feature >= HD * h) & (feature < HD * (h + 1))
                pick = jnp.where(member & (row == base + h), 1.0, 0.0).astype(BF16)
                keep = jnp.where(member[:1], 1.0, 0.0).astype(BF16)
                at = slice(HD * h - lo, HD * (h + 1) - lo)
                band[j, at, :LANES] = state * keep
                band[j, at, LANES:] = dot(sums, pick).astype(BF16)
        copies[1].wait()
        qv[...] = jnp.maximum(qv[...], 0)
        copies[2].wait()
        for j in range(TILES):
            _, _, lo, hi = heads_of(j)
            place = slice(LANES * j, LANES * (j + 1))
            both = dot(qv[:, lo:hi], band[j, : hi - lo, :])
            attn = both[:, :LANES] / (both[:, LANES:] + EPS)
            mix[:, place] = (attn + cv[:, place]).astype(BF16)

    for t in range(steps):

        @pl.when(n == t)
        def _():
            weights[t].wait()

    at = pl.ds(pl.multiple_of(256 * n, 256), 256)
    out_ref[...] = dot(mix[...], wv[:, at]).astype(BF16)


def project(q, conv, s, w):
    any_space = pl.BlockSpec(memory_space=pl.ANY)
    return pl.pallas_call(
        project_kernel,
        grid=(DP // 256,),
        out_shape=jax.ShapeDtypeStruct((TOK, D), BF16),
        in_specs=[any_space] * 4,
        out_specs=pl.BlockSpec((TOK, 256), lambda n: (0, n)),
        scratch_shapes=[
            pltpu.VMEM((TOK, D), BF16),
            pltpu.VMEM((TOK, DP), F32),
            pltpu.VMEM((16 * NZ, 16, LANES), BF16),
            pltpu.VMEM((HD, DP), BF16),
            pltpu.VMEM((TILES, 512, 256), BF16),
            pltpu.VMEM((TOK, DP), BF16),
            pltpu.VMEM((32 * BLKP, DP), BF16),
            pltpu.SemaphoreType.DMA((3 + DP // 256,)),
        ],
        compiler_params=pltpu.CompilerParams(vmem_limit_bytes=48 << 20),
        name="attend_and_project",
    )(q, conv, s, w)


def shards(queries, keys, values, conv_weight, w_out):
    q, k, v = (a.reshape(TOK, D) for a in (queries, keys, values))
    conv, states, weights = gather(k, v, w_out, conv_weight)
    return project(q, conv, states, weights).reshape(1, ROWS, COLS, D)


def solution(mesh):
    placed = P("tm", "space", None, None)
    return jax.shard_map(
        shards,
        mesh=mesh,
        in_specs=(placed, placed, placed, P(), P("tm", "space")),
        out_specs=placed,
        check_vma=False,
    )
```

```python
import functools

import jax
import jax.numpy as jnp
from jax import lax
from jax.experimental import pallas as pl
from jax.experimental.pallas import tpu as pltpu
from jax.sharding import PartitionSpec as P

HEADS = 20
HD = 112
D = HEADS * HD
ROWS, COLS = 8, 80
TOK = ROWS * COLS
LANES = 128
TILES = 18
DP = TILES * LANES
BLK, BLKP = 70, 72
UNITS = 7
NZ = 8
EPS = 1e-06
SUBS = 4
PART = 16 // SUBS
MESH = pl.DeviceIdType.MESH
F32, BF16 = jnp.float32, jnp.bfloat16


def feature_of(pos):
    return BLK * (pos // BLKP) + min(pos % BLKP, BLK - 1)


def spread_window(j):
    lo = feature_of(LANES * j) // LANES
    lo = min(lo, TILES - 2)
    return lo, LANES * lo, min(LANES * (lo + 2), D)


def spread_matrix(j, start, stop):
    shape = (stop - start, LANES)
    pos = LANES * j + lax.broadcasted_iota(jnp.int32, shape, 1)
    block = lax.shift_right_logical(pos * 14564, 20)
    inside = pos - BLKP * block
    feature = BLK * block + inside
    row = start + lax.broadcasted_iota(jnp.int32, shape, 0)
    return jnp.where((row == feature) & (inside < BLK), 1.0, 0.0).astype(BF16)


def dot(a, b):
    return jnp.dot(a, b, preferred_element_type=F32)


def add_mod(a, b, n):
    return lax.rem(a + b + 2 * n, n)


def gather_kernel(
    k_hbm, v_hbm, w_hbm, cw_hbm, conv_hbm, s_hbm, wg_hbm,
    cw_ref, kn, vn, kt, vp, cwp, conv, z_ref, fwd, bwd, own, scan, pre, xs, back, s_own, wa, wown,
    local_sem, halo_send, halo_recv, wa_send, wa_recv, rs_send, rs_recv, sc_send, sc_recv,
    xs_send, xs_recv, bk_send, bk_recv, ag_send, ag_recv, wg_send, wg_recv,
):
    tm, z = lax.axis_index("tm"), lax.axis_index("space")
    core, y, x = lax.rem(tm, 2), lax.rem(lax.div(tm, 2), 4), lax.div(tm, 8)
    member = lax.rem(tm, 8)
    dr = 1 - 2 * core

    def at(xx, yy, cc):
        return 8 * xx + 2 * yy + cc

    def along_a(k):
        other = add_mod(jnp.where(core == 0, x, y), k, 4)
        return jnp.where(core == 0, at(other, y, core), at(x, other, core))

    def along(ka, kb):
        px = add_mod(x, jnp.where(core == 0, ka, kb), 4)
        py = add_mod(y, jnp.where(core == 0, kb, ka), 4)
        return at(px, py, core)

    partner = at(x, y, 1 - core)
    everything = []

    def remote(src, dst, send, recv, to_tm, to_z):
        return pltpu.make_async_remote_copy(
            src_ref=src, dst_ref=dst, send_sem=send, recv_sem=recv,
            device_id={"tm": to_tm, "space": to_z}, device_id_type=MESH,
        )

    def start(copy):
        copy.start()
        everything.append(copy)
        return copy

    barrier = pltpu.get_barrier_semaphore()
    friends = [(tm, add_mod(z, o, NZ)) for o in range(1, NZ)]
    friends += [(8 * x + add_mod(member, o, 8), z) for o in range(1, 8)]
    friends += [(add_mod(tm, 8 * o, 32), z) for o in range(1, 4)]
    for to_tm, to_z in friends:
        pl.semaphore_signal(barrier, inc=1, device_id={"tm": to_tm, "space": to_z}, device_id_type=MESH)
    loads = [
        pltpu.make_async_copy(k_hbm, kn, local_sem.at[0]),
        pltpu.make_async_copy(v_hbm, vn.at[pl.ds(COLS, TOK)], local_sem.at[1]),
    ]
    load_cw = pltpu.make_async_copy(cw_hbm, cw_ref, local_sem.at[6])
    for copy in loads:
        copy.start()
    pl.semaphore_wait(barrier, len(friends))

    wa_mine = pltpu.make_async_copy(w_hbm, wa.at[z], local_sem.at[2])
    wa_mine.start()
    load_cw.start()
    for n, o in enumerate((1, -1, 2, -2)):
        start(remote(w_hbm, wa.at[z], wa_send.at[n], wa_recv.at[n], tm, add_mod(z, o, NZ)))
    halo = [
        remote(v_hbm.at[pl.ds(0, COLS)], vn.at[pl.ds(COLS + TOK, COLS)], halo_send.at[0], halo_recv.at[0], tm, add_mod(z, -1, NZ)),
        remote(v_hbm.at[pl.ds(TOK - COLS, COLS)], vn.at[pl.ds(0, COLS)], halo_send.at[1], halo_recv.at[1], tm, add_mod(z, 1, NZ)),
    ]

    def partial_state():
        loads[0].wait()
        for i in range(TILES):
            lo, hi = LANES * i, min(LANES * (i + 1), D)
            kt[lo:hi, :] = jnp.maximum(kn[:, lo:hi], 0).T
        loads[1].wait()
        ones = jnp.ones((TOK, LANES), BF16)
        lane = lax.broadcasted_iota(jnp.int32, (HD, LANES), 1)
        sums = jnp.zeros((HD, LANES), F32)
        for j in range(TILES):
            lo, hi = LANES * j, min(LANES * (j + 1), D)
            tile = vn[COLS : COLS + TOK, lo:hi]
            if hi - lo < LANES:
                eye = lax.broadcasted_iota(jnp.int32, (hi - lo, LANES), 0) == lax.broadcasted_iota(jnp.int32, (hi - lo, LANES), 1)
                tile = dot(tile, jnp.where(eye, 1.0, 0.0).astype(BF16)).astype(BF16)
            first, last = lo // HD, (hi - 1) // HD
            g = dot(kt[HD * first : HD * (last + 1), :], jnp.concatenate([tile, ones], axis=1))
            part = g[:HD, :LANES]
            for h in range(first, last + 1):
                rows = g[HD * (h - first) : HD * (h - first + 1)]
                part = jnp.where(lane < HD * h - lo, part, rows[:, :LANES])
                sums = jnp.where(lane == D - LANES * (TILES - 1) + h, rows[:, LANES:], sums)
            if j == TILES - 1:
                part = jnp.where(lane < D - lo, part, sums)
            for r in range(UNITS):
                z_ref[UNITS * j + r] = part[16 * r : 16 * (r + 1)]
        z_ref[UNITS * TILES] = jnp.zeros((16, LANES), F32)
        z_ref[UNITS * TILES + 1] = jnp.zeros((16, LANES), F32)

    def ring(forward, s, u):
        hops = 4 if forward else 3
        way = dr if forward else -dr
        slots = fwd if forward else bwd
        chunk = add_mod(z, way * (hops - s), NZ)
        place = pl.ds(PART * u, PART)
        sem = (0 if forward else 4 * SUBS) + SUBS * s + u
        if s == 0:
            src = z_ref.at[pl.ds(16 * chunk + PART * u, PART)]
        else:
            everything_rs[(forward, s - 1, u)].wait_recv()
            slots[s - 1, place] += z_ref[pl.ds(16 * chunk + PART * u, PART)]
            src = slots.at[s - 1, place]
        copy = remote(src, slots.at[s, place], rs_send.at[sem], rs_recv.at[sem], tm, add_mod(z, way, NZ))
        copy.start()
        everything_rs[(forward, s, u)] = copy

    everything_rs = {}

    def ring_step(s):
        for u in range(SUBS):
            ring(True, s, u)
            if s < 3:
                ring(False, s, u)

    def ring_end():
        for u in range(SUBS):
            everything_rs[(True, 3, u)].wait_recv()
            everything_rs[(False, 2, u)].wait_recv()
            place = pl.ds(PART * u, PART)
            own[place] = z_ref[pl.ds(16 * z + PART * u, PART)] + fwd[3, place] + bwd[2, place]

    def scan_send():
        for o in range(1, 8):
            other = add_mod(member, o, 8)
            start(remote(own.at[pl.ds(2 * other, 2)], scan.at[member], sc_send.at[o - 1], sc_recv.at[o - 1], 8 * x + other, z))
        scan[member] = own[pl.ds(2 * member, 2)]

    def scan_group():
        for o in range(1, 8):
            remote(own.at[pl.ds(0, 2)], scan.at[0], sc_send.at[o - 1], sc_recv.at[o - 1], tm, z).wait_recv()
        total = jnp.zeros((2, 16, LANES), F32)
        for m in range(8):
            total = total + scan[m]
            pre[m] = total
        for o in range(1, 4):
            start(remote(pre.at[7], xs.at[x], xs_send.at[o - 1], xs_recv.at[o - 1], add_mod(tm, 8 * o, 32), z))
        xs[x] = total

    def scan_back():
        for o in range(1, 4):
            remote(pre.at[7], xs.at[0], xs_send.at[o - 1], xs_recv.at[o - 1], tm, z).wait_recv()
        before = jnp.zeros((2, 16, LANES), F32)
        for k in range(4):
            before = before + jnp.where(k < x, xs[k], 0.0)
        for m in range(8):
            back[m] = (before + pre[m]).astype(BF16)
        for o in range(1, 8):
            other = add_mod(member, o, 8)
            start(remote(back.at[other], s_own.at[pl.ds(2 * member, 2)], bk_send.at[o - 1], bk_recv.at[o - 1], 8 * x + other, z))
        s_own[pl.ds(2 * member, 2)] = back[member]

    def share_state():
        for o in range(1, 8):
            remote(back.at[0], s_own.at[pl.ds(0, 2)], bk_send.at[o - 1], bk_recv.at[o - 1], tm, z).wait_recv()
        for h in range(2):
            for o in (1, -1, 2, -2):
                state_send(share_number[o] + h, s_own.at[pl.ds(8 * h, 8)], part_of(0, h), o)
        copy = pltpu.make_async_copy(s_own, s_hbm.at[pl.ds(16 * z, 16)], local_sem.at[3])
        copy.start()
        return copy

    share_number = {1: 0, -1: 2, 2: 4, -2: 6}

    def part_of(o, h):
        return s_hbm.at[pl.ds(16 * add_mod(z, o, NZ) + 8 * h, 8)]

    def state_send(n, src, dst, o):
        start(remote(src, dst, ag_send.at[n], ag_recv.at[n], tm, add_mod(z, o, NZ)))

    def state_wait(n, ref):
        remote(ref, ref, ag_send.at[n], ag_recv.at[n], tm, z).wait_recv()

    def pass_on_state():
        for h in range(2):
            state_wait(4 + h, part_of(-2, h))
            state_send(8 + h, part_of(-2, h), part_of(-2, h), 1)
            if h == 0:
                state_send(12, part_of(-2, 0), part_of(-2, 0), 2)
            state_wait(6 + h, part_of(2, h))
            state_send(10 + h, part_of(2, h), part_of(2, h), -1)
            if h == 1:
                state_send(13, part_of(2, 1), part_of(2, 1), -2)

    def state_end():
        for n, (o, h) in {0: (-1, 0), 1: (-1, 1), 2: (1, 0), 3: (1, 1)}.items():
            state_wait(n, part_of(o, h))
        for n, (o, h) in {8: (-3, 0), 9: (-3, 1), 10: (3, 0), 11: (3, 1), 12: (4, 0), 13: (4, 1)}.items():
            state_wait(n, part_of(o, h))

    def rows_of(owner, half=None):
        lo, n = (0, BLKP) if half is None else ((0, 40) if half == 0 else (40, 32))
        return wg_hbm.at[pl.ds(pl.multiple_of(BLKP * owner + lo, 8), n)]

    def w_send(n, src, dst, to_tm):
        start(remote(src, dst, wg_send.at[n], wg_recv.at[n], to_tm, z))

    def w_wait(n, ref):
        remote(ref, ref, wg_send.at[n], wg_recv.at[n], tm, z).wait_recv()

    deltas = (0, -1, 1, 2)

    def w_out_b(g, src=None):
        owner = along(deltas[g], 0)
        ref = rows_of(owner) if src is None else src
        w_send(4 + 4 * g, ref, rows_of(owner), along(0, 1))
        w_send(5 + 4 * g, ref, rows_of(owner), along(0, -1))
        w_send(20 + 4 * g, ref, rows_of(owner), partner)

    def wa_wait(n):
        remote(w_hbm, wa.at[0], wa_send.at[n], wa_recv.at[n], tm, z).wait_recv()

    def wa_pass_on():
        wa_wait(2)
        wa_wait(3)
        below, above = add_mod(z, -2, NZ), add_mod(z, 2, NZ)
        far = add_mod(z, -2 * dr, NZ)
        for n, slot, to in ((4, below, add_mod(z, 1, NZ)), (5, above, add_mod(z, -1, NZ)), (6, far, add_mod(z, 2 * dr, NZ))):
            start(remote(wa.at[slot], wa.at[slot], wa_send.at[n], wa_recv.at[n], tm, to))

    def w_assemble():
        wa_mine.wait()
        for n in (0, 1, 4, 5, 6):
            wa_wait(n)
        wown[...] = jnp.zeros((BLKP, DP), BF16)
        width = D // NZ
        for j in range(TILES):
            lo, hi = LANES * j, min(LANES * (j + 1), D)
            acc = jnp.zeros((BLK, LANES), F32)
            for b in range(lo // width, (hi - 1) // width + 1):
                row = width * b + lax.broadcasted_iota(jnp.int32, (width, LANES), 0)
                col = lo + lax.broadcasted_iota(jnp.int32, (width, LANES), 1)
                acc = acc + dot(wa[b], jnp.where(row == col, 1.0, 0.0).astype(BF16))
            wown[0:BLK, lo : lo + LANES] = acc.astype(BF16)
        mine = pltpu.make_async_copy(wown, rows_of(tm), local_sem.at[4])
        mine.start()
        w_send(0, wown, rows_of(tm), along(1, 0))
        w_send(1, wown, rows_of(tm), along(-1, 0))
        return mine

    def w_pass_full():
        low, high = along(-1, 0), along(1, 0)
        w_wait(0, rows_of(low))
        w_wait(1, rows_of(high))
        w_send(2, rows_of(low, 0), rows_of(low, 0), high)
        w_send(3, rows_of(high, 1), rows_of(high, 1), low)

    def w_wait_half():
        w_wait(2, rows_of(along(2, 0), 0))
        w_wait(3, rows_of(along(2, 0), 1))

    def w_b_full(g):
        low, high = along(deltas[g], -1), along(deltas[g], 1)
        w_wait(4 + 4 * g, rows_of(low))
        w_send(6 + 4 * g, rows_of(low, 0), rows_of(low, 0), along(0, 1))
        w_wait(5 + 4 * g, rows_of(high))
        w_send(7 + 4 * g, rows_of(high, 1), rows_of(high, 1), along(0, -1))
        w_send(21 + 4 * g, rows_of(low), rows_of(low), partner)
        w_send(22 + 4 * g, rows_of(high), rows_of(high), partner)

    def w_b_half(g):
        far = along(deltas[g], 2)
        w_wait(6 + 4 * g, rows_of(far, 0))
        w_wait(7 + 4 * g, rows_of(far, 1))
        w_send(23 + 4 * g, rows_of(far), rows_of(far), partner)

    def w_end():
        for n in range(20, 36):
            w_wait(n, rows_of(0))

    def conv_prepare():
        load_cw.wait()
        for j in range(TILES):
            _, lo, hi = spread_window(j)
            spread = spread_matrix(j, lo, hi)
            place = slice(LANES * j, LANES * (j + 1))
            vp[COLS : COLS + TOK, place] = dot(vn[COLS : COLS + TOK, lo:hi], spread).astype(BF16)
            for a in range(3):
                rest = cw_ref[a, :, lo:hi]
                total = jnp.zeros((3, LANES), F32)
                for _ in range(3):
                    piece = rest.astype(BF16)
                    total = total + dot(piece, spread)
                    rest = rest - piece.astype(F32)
                cwp[a, 0:3, place] = total

    def conv_rims():
        for copy in halo:
            copy.wait_recv()
        for n, start_row in enumerate((0, COLS + TOK)):
            there = jnp.where(z == (0, NZ - 1)[n], 0.0, 1.0)
            for j in range(TILES):
                _, lo, hi = spread_window(j)
                rim = dot(vn[start_row : start_row + COLS, lo:hi], spread_matrix(j, lo, hi))
                vp[start_row : start_row + COLS, LANES * j : LANES * (j + 1)] = (rim * there).astype(BF16)

    def conv_rows(first, last):
        row = lax.broadcasted_iota(jnp.int32, (COLS, LANES), 0)

        @pl.loop(first, last)
        def _(r):
            base = pl.multiple_of(COLS * r, 16)
            for j in range(TILES):
                place = slice(LANES * j, LANES * (j + 1))
                lines = [vp[pl.ds(base + COLS * a, COLS), place].astype(F32) for a in range(3)]
                sums = []
                for b in range(3):
                    sums.append(sum(lines[a] * cwp[a, b : b + 1, place] for a in range(3)))
                left = jnp.where(row == 0, 0.0, pltpu.roll(sums[0], 1, 0))
                right = jnp.where(row == COLS - 1, 0.0, pltpu.roll(sums[2], COLS - 1, 0))
                conv[pl.ds(base, COLS), place] = sums[1] + left + right

    partial_state()
    ring_step(0)
    wa_pass_on()
    conv_prepare()
    ring_step(1)
    ring_step(2)
    mine = w_assemble()
    ring_step(3)
    for copy in halo:
        start(copy)
    w_out_b(0, wown)
    conv_rows(1, 4)
    ring_end()
    scan_send()
    w_pass_full()
    conv_rows(4, 6)
    scan_group()
    w_out_b(1)
    w_b_full(0)
    conv_rows(6, 7)
    scan_back()
    w_out_b(2)
    state_mine = share_state()
    w_wait_half()
    w_out_b(3)
    conv_rims()
    conv_rows(0, 1)
    conv_rows(7, 8)
    conv_out = pltpu.make_async_copy(conv, conv_hbm, local_sem.at[5])
    conv_out.start()
    pass_on_state()
    mine.wait()
    w_b_half(0)
    w_b_full(1)
    w_b_full(2)
    w_b_full(3)
    w_b_half(1)
    w_b_half(2)
    w_b_half(3)
    state_end()
    w_end()
    for copy in everything + list(everything_rs.values()):
        copy.wait_send()
    state_mine.wait()
    conv_out.wait()


def gather(k, v, w, cw):
    dma = pltpu.SemaphoreType.DMA
    any_space = pl.BlockSpec(memory_space=pl.ANY)
    return pl.pallas_call(
        gather_kernel,
        out_shape=(
            jax.ShapeDtypeStruct((TOK, DP), F32),
            jax.ShapeDtypeStruct((16 * NZ, 16, LANES), BF16),
            jax.ShapeDtypeStruct((32 * BLKP, DP), BF16),
        ),
        in_specs=[pl.BlockSpec(memory_space=pltpu.HBM)] * 4,
        out_specs=(any_space,) * 3,
        scratch_shapes=[
            pltpu.VMEM((3, 3, D), F32),
            pltpu.VMEM((TOK, D), BF16),
            pltpu.VMEM((TOK + 2 * COLS, D), BF16),
            pltpu.VMEM((D, TOK), BF16),
            pltpu.VMEM((TOK + 2 * COLS, DP), BF16),
            pltpu.VMEM((3, 8, DP), F32),
            pltpu.VMEM((TOK, DP), F32),
            pltpu.VMEM((16 * NZ, 16, LANES), F32),
            pltpu.VMEM((4, 16, 16, LANES), F32),
            pltpu.VMEM((3, 16, 16, LANES), F32),
            pltpu.VMEM((16, 16, LANES), F32),
            pltpu.VMEM((8, 2, 16, LANES), F32),
            pltpu.VMEM((8, 2, 16, LANES), F32),
            pltpu.VMEM((4, 2, 16, LANES), F32),
            pltpu.VMEM((8, 2, 16, LANES), BF16),
            pltpu.VMEM((16, 16, LANES), BF16),
            pltpu.VMEM((NZ, BLK, D // NZ), BF16),
            pltpu.VMEM((BLKP, DP), BF16),
            dma((7,)), dma((2,)), dma((2,)), dma((7,)), dma((7,)), dma((7 * SUBS,)), dma((7 * SUBS,)),
            dma((7,)), dma((7,)), dma((3,)), dma((3,)), dma((7,)), dma((7,)), dma((14,)), dma((14,)),
            dma((36,)), dma((36,)),
        ],
        compiler_params=pltpu.CompilerParams(
            collective_id=0, has_side_effects=True, vmem_limit_bytes=60 << 20
        ),
        name="state_and_gather",
    )(k, v, w, cw)


def heads_of(j):
    features = [
        feature_of(p) for p in range(LANES * j, LANES * (j + 1)) if p % BLKP < BLK
    ]
    first, last = min(features) // HD, max(features) // HD
    lo = HD * first // LANES * LANES
    hi = min(-(-HD * (last + 1) // LANES) * LANES, D)
    return first, last, lo, hi


def project_kernel(q_hbm, conv_hbm, s_hbm, w_hbm, out_ref, qv, cv, sv, sn, band, mix, wv, sem):
    n = pl.program_id(0)
    steps = DP // 256
    copies = [
        pltpu.make_async_copy(s_hbm, sv, sem.at[0]),
        pltpu.make_async_copy(q_hbm, qv, sem.at[1]),
        pltpu.make_async_copy(conv_hbm, cv, sem.at[2]),
    ]
    weights = [
        pltpu.make_async_copy(
            w_hbm.at[:, pl.ds(256 * t, 256)], wv.at[:, pl.ds(256 * t, 256)], sem.at[3 + t]
        )
        for t in range(steps)
    ]

    @pl.when(n == 0)
    def _():
        for copy in copies + weights:
            copy.start()
        copies[0].wait()
        for j in range(TILES):
            for r in range(UNITS):
                sn[16 * r : 16 * (r + 1), LANES * j : LANES * (j + 1)] = sv[UNITS * j + r]
        sums = sn[:, LANES * (TILES - 1) :]
        base = D - LANES * (TILES - 1)
        for j in range(TILES):
            first, last, lo, hi = heads_of(j)
            band[j] = jnp.zeros(band.shape[1:], BF16)
            _, w_lo, _ = spread_window(j)
            w_hi = w_lo + 2 * LANES
            spread = spread_matrix(j, w_lo, w_hi)
            state = dot(sn[:, w_lo:w_hi], spread).astype(BF16)
            pos = LANES * j + lax.broadcasted_iota(jnp.int32, (LANES, LANES), 1)
            block = lax.shift_right_logical(pos * 14564, 20)
            inside = pos - BLKP * block
            feature = BLK * block + inside
            row = lax.broadcasted_iota(jnp.int32, (LANES, LANES), 0)
            for h in range(first, last + 1):
                member = (inside < BLK) & (feature >= HD * h) & (feature < HD * (h + 1))
                pick = jnp.where(member & (row == base + h), 1.0, 0.0).astype(BF16)
                keep = jnp.where(member[:1], 1.0, 0.0).astype(BF16)
                at = slice(HD * h - lo, HD * (h + 1) - lo)
                band[j, at, :LANES] = state * keep
                band[j, at, LANES:] = dot(sums, pick).astype(BF16)
        copies[1].wait()
        qv[...] = jnp.maximum(qv[...], 0)
        copies[2].wait()
        for j in range(TILES):
            _, _, lo, hi = heads_of(j)
            place = slice(LANES * j, LANES * (j + 1))
            both = dot(qv[:, lo:hi], band[j, : hi - lo, :])
            attn = both[:, :LANES] / (both[:, LANES:] + EPS)
            mix[:, place] = (attn + cv[:, place]).astype(BF16)

    for t in range(steps):

        @pl.when(n == t)
        def _():
            weights[t].wait()

    at = pl.ds(pl.multiple_of(256 * n, 256), 256)
    out_ref[...] = dot(mix[...], wv[:, at]).astype(BF16)


def project(q, conv, s, w):
    any_space = pl.BlockSpec(memory_space=pl.ANY)
    return pl.pallas_call(
        project_kernel,
        grid=(DP // 256,),
        out_shape=jax.ShapeDtypeStruct((TOK, D), BF16),
        in_specs=[pl.BlockSpec(memory_space=pltpu.HBM)] + [any_space] * 3,
        out_specs=pl.BlockSpec((TOK, 256), lambda n: (0, n)),
        scratch_shapes=[
            pltpu.VMEM((TOK, D), BF16),
            pltpu.VMEM((TOK, DP), F32),
            pltpu.VMEM((16 * NZ, 16, LANES), BF16),
            pltpu.VMEM((HD, DP), BF16),
            pltpu.VMEM((TILES, 512, 256), BF16),
            pltpu.VMEM((TOK, DP), BF16),
            pltpu.VMEM((32 * BLKP, DP), BF16),
            pltpu.SemaphoreType.DMA((3 + DP // 256,)),
        ],
        compiler_params=pltpu.CompilerParams(vmem_limit_bytes=48 << 20),
        name="attend_and_project",
    )(q, conv, s, w)


def shards(queries, keys, values, conv_weight, w_out):
    q, k, v = (a.reshape(TOK, D) for a in (queries, keys, values))
    conv, states, weights = gather(k, v, w_out, conv_weight)
    return project(q, conv, states, weights).reshape(1, ROWS, COLS, D)


def solution(mesh):
    placed = P("tm", "space", None, None)
    return jax.shard_map(
        shards,
        mesh=mesh,
        in_specs=(placed, placed, placed, P(), P("tm", "space")),
        out_specs=placed,
        check_vma=False,
    )
```

```python
import functools

import jax
import jax.numpy as jnp
from jax import lax
from jax.experimental import pallas as pl
from jax.experimental.pallas import tpu as pltpu
from jax.sharding import PartitionSpec as P

HEADS = 20
HD = 112
D = HEADS * HD
ROWS, COLS = 8, 80
TOK = ROWS * COLS
LANES = 128
TILES = 18
DP = TILES * LANES
BLK, BLKP = 70, 72
UNITS = 7
NZ = 8
EPS = 1e-06
FIRST = 1280
SUBS = 4
PART = 16 // SUBS
MESH = pl.DeviceIdType.MESH
F32, BF16 = jnp.float32, jnp.bfloat16


def feature_of(pos):
    return BLK * (pos // BLKP) + min(pos % BLKP, BLK - 1)


def spread_window(j):
    lo = feature_of(LANES * j) // LANES
    lo = min(lo, TILES - 2)
    return lo, LANES * lo, min(LANES * (lo + 2), D)


def spread_matrix(j, start, stop):
    shape = (stop - start, LANES)
    pos = LANES * j + lax.broadcasted_iota(jnp.int32, shape, 1)
    block = lax.shift_right_logical(pos * 14564, 20)
    inside = pos - BLKP * block
    feature = BLK * block + inside
    row = start + lax.broadcasted_iota(jnp.int32, shape, 0)
    return jnp.where((row == feature) & (inside < BLK), 1.0, 0.0).astype(BF16)


def dot(a, b):
    return jnp.dot(a, b, preferred_element_type=F32)


def add_mod(a, b, n):
    return lax.rem(a + b + 2 * n, n)


def gather_kernel(
    q_hbm, k_hbm, v_hbm, w_hbm, cw_hbm, out_hbm, wg_hbm,
    cw_ref, kn, vn, kt, vp, cwp, conv, z_ref, fwd, bwd, own, scan, pre, xs, back, s_own, wa, wown,
    s_all, sn, band, spreads, picks, qv, mix, wv, out_v,
    local_sem, halo_send, halo_recv, wa_send, wa_recv, rs_send, rs_recv, sc_send, sc_recv,
    xs_send, xs_recv, bk_send, bk_recv, ag_send, ag_recv, wg_send, wg_recv,
):
    tm, z = lax.axis_index("tm"), lax.axis_index("space")
    core, y, x = lax.rem(tm, 2), lax.rem(lax.div(tm, 2), 4), lax.div(tm, 8)
    member = lax.rem(tm, 8)
    dr = 1 - 2 * core

    def at(xx, yy, cc):
        return 8 * xx + 2 * yy + cc

    def along_a(k):
        other = add_mod(jnp.where(core == 0, x, y), k, 4)
        return jnp.where(core == 0, at(other, y, core), at(x, other, core))

    def along(ka, kb):
        px = add_mod(x, jnp.where(core == 0, ka, kb), 4)
        py = add_mod(y, jnp.where(core == 0, kb, ka), 4)
        return at(px, py, core)

    partner = at(x, y, 1 - core)
    everything = []

    def remote(src, dst, send, recv, to_tm, to_z):
        return pltpu.make_async_remote_copy(
            src_ref=src, dst_ref=dst, send_sem=send, recv_sem=recv,
            device_id={"tm": to_tm, "space": to_z}, device_id_type=MESH,
        )

    def start(copy):
        copy.start()
        everything.append(copy)
        return copy

    barrier = pltpu.get_barrier_semaphore()
    friends = [(tm, add_mod(z, o, NZ)) for o in range(1, NZ)]
    friends += [(8 * x + add_mod(member, o, 8), z) for o in range(1, 8)]
    friends += [(add_mod(tm, 8 * o, 32), z) for o in range(1, 4)]
    for to_tm, to_z in friends:
        pl.semaphore_signal(barrier, inc=1, device_id={"tm": to_tm, "space": to_z}, device_id_type=MESH)
    loads = [
        pltpu.make_async_copy(k_hbm, kn, local_sem.at[0]),
        pltpu.make_async_copy(v_hbm, vn.at[pl.ds(COLS, TOK)], local_sem.at[1]),
    ]
    load_cw = pltpu.make_async_copy(cw_hbm, cw_ref, local_sem.at[6])
    for copy in loads:
        copy.start()
    pl.semaphore_wait(barrier, len(friends))

    wa_mine = pltpu.make_async_copy(w_hbm, wa.at[z], local_sem.at[2])
    wa_mine.start()
    load_cw.start()
    for n, o in enumerate((1, -1, 2, -2)):
        start(remote(w_hbm, wa.at[z], wa_send.at[n], wa_recv.at[n], tm, add_mod(z, o, NZ)))
    halo = [
        remote(v_hbm.at[pl.ds(0, COLS)], vn.at[pl.ds(COLS + TOK, COLS)], halo_send.at[0], halo_recv.at[0], tm, add_mod(z, -1, NZ)),
        remote(v_hbm.at[pl.ds(TOK - COLS, COLS)], vn.at[pl.ds(0, COLS)], halo_send.at[1], halo_recv.at[1], tm, add_mod(z, 1, NZ)),
    ]

    def partial_state():
        loads[0].wait()
        for i in range(TILES):
            lo, hi = LANES * i, min(LANES * (i + 1), D)
            kt[lo:hi, :] = jnp.maximum(kn[:, lo:hi], 0).T
        loads[1].wait()
        ones = jnp.ones((TOK, LANES), BF16)
        lane = lax.broadcasted_iota(jnp.int32, (HD, LANES), 1)
        sums = jnp.zeros((HD, LANES), F32)
        for j in range(TILES):
            lo, hi = LANES * j, min(LANES * (j + 1), D)
            tile = vn[COLS : COLS + TOK, lo:hi]
            if hi - lo < LANES:
                eye = lax.broadcasted_iota(jnp.int32, (hi - lo, LANES), 0) == lax.broadcasted_iota(jnp.int32, (hi - lo, LANES), 1)
                tile = dot(tile, jnp.where(eye, 1.0, 0.0).astype(BF16)).astype(BF16)
            first, last = lo // HD, (hi - 1) // HD
            g = dot(kt[HD * first : HD * (last + 1), :], jnp.concatenate([tile, ones], axis=1))
            part = g[:HD, :LANES]
            for h in range(first, last + 1):
                rows = g[HD * (h - first) : HD * (h - first + 1)]
                part = jnp.where(lane < HD * h - lo, part, rows[:, :LANES])
                sums = jnp.where(lane == D - LANES * (TILES - 1) + h, rows[:, LANES:], sums)
            if j == TILES - 1:
                part = jnp.where(lane < D - lo, part, sums)
            for r in range(UNITS):
                z_ref[UNITS * j + r] = part[16 * r : 16 * (r + 1)]
        z_ref[UNITS * TILES] = jnp.zeros((16, LANES), F32)
        z_ref[UNITS * TILES + 1] = jnp.zeros((16, LANES), F32)

    def ring(forward, s, u):
        hops = 4 if forward else 3
        way = dr if forward else -dr
        slots = fwd if forward else bwd
        chunk = add_mod(z, way * (hops - s), NZ)
        place = pl.ds(PART * u, PART)
        sem = (0 if forward else 4 * SUBS) + SUBS * s + u
        if s == 0:
            src = z_ref.at[pl.ds(16 * chunk + PART * u, PART)]
        else:
            everything_rs[(forward, s - 1, u)].wait_recv()
            slots[s - 1, place] += z_ref[pl.ds(16 * chunk + PART * u, PART)]
            src = slots.at[s - 1, place]
        copy = remote(src, slots.at[s, place], rs_send.at[sem], rs_recv.at[sem], tm, add_mod(z, way, NZ))
        copy.start()
        everything_rs[(forward, s, u)] = copy

    everything_rs = {}

    def ring_step(s):
        for u in range(SUBS):
            ring(True, s, u)
            if s < 3:
                ring(False, s, u)

    def ring_end():
        for u in range(SUBS):
            everything_rs[(True, 3, u)].wait_recv()
            everything_rs[(False, 2, u)].wait_recv()
            place = pl.ds(PART * u, PART)
            own[place] = z_ref[pl.ds(16 * z + PART * u, PART)] + fwd[3, place] + bwd[2, place]

    def scan_send():
        for o in range(1, 8):
            other = add_mod(member, o, 8)
            start(remote(own.at[pl.ds(2 * other, 2)], scan.at[member], sc_send.at[o - 1], sc_recv.at[o - 1], 8 * x + other, z))
        scan[member] = own[pl.ds(2 * member, 2)]

    def scan_group():
        for o in range(1, 8):
            remote(own.at[pl.ds(0, 2)], scan.at[0], sc_send.at[o - 1], sc_recv.at[o - 1], tm, z).wait_recv()
        total = jnp.zeros((2, 16, LANES), F32)
        for m in range(8):
            total = total + scan[m]
            pre[m] = total
        for o in range(1, 4):
            start(remote(pre.at[7], xs.at[x], xs_send.at[o - 1], xs_recv.at[o - 1], add_mod(tm, 8 * o, 32), z))
        xs[x] = total

    def scan_back():
        for o in range(1, 4):
            remote(pre.at[7], xs.at[0], xs_send.at[o - 1], xs_recv.at[o - 1], tm, z).wait_recv()
        before = jnp.zeros((2, 16, LANES), F32)
        for k in range(4):
            before = before + jnp.where(k < x, xs[k], 0.0)
        for m in range(8):
            back[m] = (before + pre[m]).astype(BF16)
        for o in range(1, 8):
            other = add_mod(member, o, 8)
            start(remote(back.at[other], s_own.at[pl.ds(2 * member, 2)], bk_send.at[o - 1], bk_recv.at[o - 1], 8 * x + other, z))
        s_own[pl.ds(2 * member, 2)] = back[member]

    def share_state():
        for o in range(1, 8):
            remote(back.at[0], s_own.at[pl.ds(0, 2)], bk_send.at[o - 1], bk_recv.at[o - 1], tm, z).wait_recv()
        for h in range(2):
            for o in (1, -1, 2, -2):
                state_send(share_number[o] + h, s_own.at[pl.ds(8 * h, 8)], part_of(0, h), o)
        copy = pltpu.make_async_copy(s_own, s_all.at[pl.ds(16 * z, 16)], local_sem.at[3])
        copy.start()
        return copy

    share_number = {1: 0, -1: 2, 2: 4, -2: 6}

    def part_of(o, h):
        return s_all.at[pl.ds(16 * add_mod(z, o, NZ) + 8 * h, 8)]

    def state_send(n, src, dst, o):
        start(remote(src, dst, ag_send.at[n], ag_recv.at[n], tm, add_mod(z, o, NZ)))

    def state_wait(n, ref):
        remote(ref, ref, ag_send.at[n], ag_recv.at[n], tm, z).wait_recv()

    def pass_on_state():
        for h in range(2):
            state_wait(4 + h, part_of(-2, h))
            state_send(8 + h, part_of(-2, h), part_of(-2, h), 1)
            if h == 0:
                state_send(12, part_of(-2, 0), part_of(-2, 0), 2)
            state_wait(6 + h, part_of(2, h))
            state_send(10 + h, part_of(2, h), part_of(2, h), -1)
            if h == 1:
                state_send(13, part_of(2, 1), part_of(2, 1), -2)

    def state_end():
        for n, (o, h) in {0: (-1, 0), 1: (-1, 1), 2: (1, 0), 3: (1, 1)}.items():
            state_wait(n, part_of(o, h))
        for n, (o, h) in {8: (-3, 0), 9: (-3, 1), 10: (3, 0), 11: (3, 1), 12: (4, 0), 13: (4, 1)}.items():
            state_wait(n, part_of(o, h))

    def rows_of(owner, half=None, p=0):
        lo, n = (0, BLKP) if half is None else ((0, 40) if half == 0 else (40, 32))
        return wg_hbm.at[pl.ds(pl.multiple_of(BLKP * owner + lo, 8), n), columns(p)]

    def columns(p):
        return pl.ds(0, FIRST) if p == 0 else pl.ds(FIRST, DP - FIRST)

    def w_send(n, src, dst, to_tm, p):
        start(remote(src, dst, wg_send.at[36 * p + n], wg_recv.at[36 * p + n], to_tm, z))

    def w_wait(n, ref, p):
        remote(ref, ref, wg_send.at[36 * p + n], wg_recv.at[36 * p + n], tm, z).wait_recv()

    deltas = (0, -1, 1, 2)

    def w_out_b(g, p):
        owner = along(deltas[g], 0)
        ref = rows_of(owner, p=p) if g else wown.at[:, columns(p)]
        to = rows_of(owner, p=p)
        w_send(4 + 4 * g, ref, to, along(0, 1), p)
        w_send(5 + 4 * g, ref, to, along(0, -1), p)
        w_send(20 + 4 * g, ref, to, partner, p)

    def wa_wait(n):
        remote(w_hbm, wa.at[0], wa_send.at[n], wa_recv.at[n], tm, z).wait_recv()

    def wa_pass_on():
        wa_wait(2)
        wa_wait(3)
        below, above = add_mod(z, -2, NZ), add_mod(z, 2, NZ)
        far = add_mod(z, -2 * dr, NZ)
        for n, slot, to in ((4, below, add_mod(z, 1, NZ)), (5, above, add_mod(z, -1, NZ)), (6, far, add_mod(z, 2 * dr, NZ))):
            start(remote(wa.at[slot], wa.at[slot], wa_send.at[n], wa_recv.at[n], tm, to))

    def w_assemble():
        wa_mine.wait()
        for n in (0, 1, 4, 5, 6):
            wa_wait(n)
        wown[...] = jnp.zeros((BLKP, DP), BF16)
        width = D // NZ
        for j in range(TILES):
            lo, hi = LANES * j, min(LANES * (j + 1), D)
            acc = jnp.zeros((BLK, LANES), F32)
            for b in range(lo // width, (hi - 1) // width + 1):
                row = width * b + lax.broadcasted_iota(jnp.int32, (width, LANES), 0)
                col = lo + lax.broadcasted_iota(jnp.int32, (width, LANES), 1)
                acc = acc + dot(wa[b], jnp.where(row == col, 1.0, 0.0).astype(BF16))
            wown[0:BLK, lo : lo + LANES] = acc.astype(BF16)
        mine = [
            pltpu.make_async_copy(wown.at[:, columns(p)], rows_of(tm, p=p), local_sem.at[(4, 10)[p]])
            for p in range(2)
        ]
        for copy in mine:
            copy.start()
        return mine

    def w_out_a(p):
        for n, k in enumerate((1, -1)):
            w_send(n, wown.at[:, columns(p)], rows_of(tm, p=p), along(k, 0), p)

    def w_pass_full(p):
        low, high = along(-1, 0), along(1, 0)
        w_wait(0, rows_of(low, p=p), p)
        w_wait(1, rows_of(high, p=p), p)
        w_send(2, rows_of(low, 0, p), rows_of(low, 0, p), high, p)
        w_send(3, rows_of(high, 1, p), rows_of(high, 1, p), low, p)

    def w_wait_half(p):
        w_wait(2, rows_of(along(2, 0), 0, p), p)
        w_wait(3, rows_of(along(2, 0), 1, p), p)

    def w_b_full(g, p):
        low, high = along(deltas[g], -1), along(deltas[g], 1)
        w_wait(4 + 4 * g, rows_of(low, p=p), p)
        w_send(6 + 4 * g, rows_of(low, 0, p), rows_of(low, 0, p), along(0, 1), p)
        w_wait(5 + 4 * g, rows_of(high, p=p), p)
        w_send(7 + 4 * g, rows_of(high, 1, p), rows_of(high, 1, p), along(0, -1), p)
        w_send(21 + 4 * g, rows_of(low, p=p), rows_of(low, p=p), partner, p)
        w_send(22 + 4 * g, rows_of(high, p=p), rows_of(high, p=p), partner, p)

    def w_b_half(g, p):
        far = along(deltas[g], 2)
        w_wait(6 + 4 * g, rows_of(far, 0, p), p)
        w_wait(7 + 4 * g, rows_of(far, 1, p), p)
        w_send(23 + 4 * g, rows_of(far, p=p), rows_of(far, p=p), partner, p)

    def w_end(p):
        for n in range(20, 36):
            w_wait(n, rows_of(0, p=p), p)

    def conv_prepare():
        load_cw.wait()
        for j in range(TILES):
            _, lo, hi = spread_window(j)
            spread = spreads[j, : hi - lo, :]
            place = slice(LANES * j, LANES * (j + 1))
            vp[COLS : COLS + TOK, place] = dot(vn[COLS : COLS + TOK, lo:hi], spread).astype(BF16)
            for a in range(3):
                rest = cw_ref[a, :, lo:hi]
                total = jnp.zeros((3, LANES), F32)
                for _ in range(3):
                    piece = rest.astype(BF16)
                    total = total + dot(piece, spread)
                    rest = rest - piece.astype(F32)
                cwp[a, 0:3, place] = total

    def conv_rims():
        for copy in halo:
            copy.wait_recv()
        for n, start_row in enumerate((0, COLS + TOK)):
            there = jnp.where(z == (0, NZ - 1)[n], 0.0, 1.0)
            for j in range(TILES):
                _, lo, hi = spread_window(j)
                rim = dot(vn[start_row : start_row + COLS, lo:hi], spreads[j, : hi - lo, :])
                vp[start_row : start_row + COLS, LANES * j : LANES * (j + 1)] = (rim * there).astype(BF16)

    def conv_rows(first, last):
        row = lax.broadcasted_iota(jnp.int32, (COLS, LANES), 0)

        @pl.loop(first, last)
        def _(r):
            base = pl.multiple_of(COLS * r, 16)
            for j in range(TILES):
                place = slice(LANES * j, LANES * (j + 1))
                lines = [vp[pl.ds(base + COLS * a, COLS), place].astype(F32) for a in range(3)]
                sums = []
                for b in range(3):
                    sums.append(sum(lines[a] * cwp[a, b : b + 1, place] for a in range(3)))
                left = jnp.where(row == 0, 0.0, pltpu.roll(sums[0], 1, 0))
                right = jnp.where(row == COLS - 1, 0.0, pltpu.roll(sums[2], COLS - 1, 0))
                conv[pl.ds(base, COLS), place] = sums[1] + left + right

    def make_masks():
        base = D - LANES * (TILES - 1)
        pos = lax.broadcasted_iota(jnp.int32, (LANES, LANES), 1)
        row = lax.broadcasted_iota(jnp.int32, (LANES, LANES), 0)
        for j in range(TILES):
            _, lo, _ = spread_window(j)
            spreads[j] = spread_matrix(j, lo, lo + 2 * LANES)
        n = 0
        for j in range(TILES):
            for h, from_lane, to_lane in head_lanes(j):
                at = (pos >= from_lane) & (pos < to_lane) & (row == base + h)
                picks[n] = jnp.where(at, 1.0, 0.0).astype(BF16)
                n += 1

    def clear_bands():
        for j in range(TILES):
            band[j] = jnp.zeros(band.shape[1:], BF16)

    def make_bands():
        for j in range(TILES):
            for r in range(UNITS):
                sn[16 * r : 16 * (r + 1), LANES * j : LANES * (j + 1)] = s_all[UNITS * j + r]
        sums = sn[:, LANES * (TILES - 1) :]
        lane = lax.broadcasted_iota(jnp.int32, (1, LANES), 1)
        n = 0
        for j in range(TILES):
            _, _, lo, _ = heads_of(j)
            _, w_lo, _ = spread_window(j)
            state = dot(sn[:, w_lo : w_lo + 2 * LANES], spreads[j]).astype(BF16)
            for h, from_lane, to_lane in head_lanes(j):
                keep = jnp.where((lane >= from_lane) & (lane < to_lane), 1.0, 0.0).astype(BF16)
                at = slice(HD * h - lo, HD * (h + 1) - lo)
                band[j, at, :LANES] = state * keep
                band[j, at, LANES:] = dot(sums, picks[n]).astype(BF16)
                n += 1

    def attend(tiles):
        for j in tiles:
            _, _, lo, hi = heads_of(j)
            place = slice(LANES * j, LANES * (j + 1))
            both = dot(jnp.maximum(qv[:, lo:hi], 0), band[j, : hi - lo, :])
            mix[:, place] = (both[:, :LANES] / (both[:, LANES:] + EPS) + conv[:, place]).astype(BF16)

    def project(lo, hi):
        @pl.loop(lo, hi)
        def _(n):
            at = pl.ds(pl.multiple_of(256 * n, 256), 256)
            out_v[:, at] = dot(mix[...], wv[:, at]).astype(BF16)

    load_q = pltpu.make_async_copy(q_hbm, qv, local_sem.at[7])
    load_w = [
        pltpu.make_async_copy(wg_hbm.at[:, columns(p)], wv.at[:, columns(p)], local_sem.at[(8, 5)[p]])
        for p in range(2)
    ]
    save_out = [
        pltpu.make_async_copy(out_v.at[:, columns(p)], out_hbm.at[:, columns(p)], local_sem.at[(9, 11)[p]])
        for p in range(2)
    ]

    partial_state()
    ring_step(0)
    load_q.start()
    make_masks()
    ring_step(1)
    wa_pass_on()
    conv_prepare()
    clear_bands()
    ring_step(2)
    mine = w_assemble()
    w_out_a(0)
    w_out_b(0, 0)
    w_out_a(1)
    ring_step(3)
    for copy in halo:
        start(copy)
    conv_rows(1, 4)
    ring_end()
    scan_send()
    w_pass_full(0)
    w_out_b(1, 0)
    w_b_full(0, 0)
    conv_rows(4, 6)
    scan_group()
    w_out_b(2, 0)
    w_pass_full(1)
    conv_rows(6, 7)
    scan_back()
    w_wait_half(0)
    w_out_b(3, 0)
    w_out_b(0, 1)
    state_mine = share_state()
    w_b_full(1, 0)
    w_b_half(0, 0)
    w_out_b(1, 1)
    conv_rims()
    conv_rows(0, 1)
    conv_rows(7, 8)
    pass_on_state()
    w_b_full(2, 0)
    w_b_full(3, 0)
    w_b_full(0, 1)
    w_out_b(2, 1)
    w_wait_half(1)
    w_out_b(3, 1)
    state_end()
    state_mine.wait()
    w_b_half(1, 0)
    w_b_half(2, 0)
    w_b_full(1, 1)
    make_bands()
    w_b_half(3, 0)
    w_b_full(2, 1)
    load_q.wait()
    attend(range(0, 5))
    for copy in mine:
        copy.wait()
    w_end(0)
    load_w[0].start()
    w_b_full(3, 1)
    attend(range(5, TILES))
    w_b_half(0, 1)
    w_b_half(1, 1)
    load_w[0].wait()
    project(0, 1)
    w_b_half(2, 1)
    w_b_half(3, 1)
    project(1, 3)
    w_end(1)
    load_w[1].start()
    project(3, 5)
    save_out[0].start()
    load_w[1].wait()
    project(5, 9)
    save_out[1].start()
    for copy in everything + list(everything_rs.values()):
        copy.wait_send()
    for copy in save_out:
        copy.wait()


def head_lanes(j):
    heads = {}
    for lane in range(LANES):
        heads.setdefault(feature_of(LANES * j + lane) // HD, []).append(lane)
    return [(h, min(lanes), max(lanes) + 1) for h, lanes in sorted(heads.items())]


def gather(q, k, v, w, cw):
    dma = pltpu.SemaphoreType.DMA
    any_space = pl.BlockSpec(memory_space=pl.ANY)
    return pl.pallas_call(
        gather_kernel,
        out_shape=(
            jax.ShapeDtypeStruct((TOK, DP), BF16),
            jax.ShapeDtypeStruct((32 * BLKP, DP), BF16),
        ),
        in_specs=[pl.BlockSpec(memory_space=pltpu.HBM)] * 5,
        out_specs=(any_space,) * 2,
        scratch_shapes=[
            pltpu.VMEM((3, 3, D), F32),
            pltpu.VMEM((TOK, D), BF16),
            pltpu.VMEM((TOK + 2 * COLS, D), BF16),
            pltpu.VMEM((D, TOK), BF16),
            pltpu.VMEM((TOK + 2 * COLS, DP), BF16),
            pltpu.VMEM((3, 8, DP), F32),
            pltpu.VMEM((TOK, DP), F32),
            pltpu.VMEM((16 * NZ, 16, LANES), F32),
            pltpu.VMEM((4, 16, 16, LANES), F32),
            pltpu.VMEM((3, 16, 16, LANES), F32),
            pltpu.VMEM((16, 16, LANES), F32),
            pltpu.VMEM((8, 2, 16, LANES), F32),
            pltpu.VMEM((8, 2, 16, LANES), F32),
            pltpu.VMEM((4, 2, 16, LANES), F32),
            pltpu.VMEM((8, 2, 16, LANES), BF16),
            pltpu.VMEM((16, 16, LANES), BF16),
            pltpu.VMEM((NZ, BLK, D // NZ), BF16),
            pltpu.VMEM((BLKP, DP), BF16),
            pltpu.VMEM((16 * NZ, 16, LANES), BF16),
            pltpu.VMEM((HD, DP), BF16),
            pltpu.VMEM((TILES, 512, 256), BF16),
            pltpu.VMEM((TILES, 256, LANES), BF16),
            pltpu.VMEM((sum(len(head_lanes(j)) for j in range(TILES)), LANES, LANES), BF16),
            pltpu.VMEM((TOK, D), BF16),
            pltpu.VMEM((TOK, DP), BF16),
            pltpu.VMEM((32 * BLKP, DP), BF16),
            pltpu.VMEM((TOK, DP), BF16),
            dma((12,)), dma((2,)), dma((2,)), dma((7,)), dma((7,)), dma((7 * SUBS,)), dma((7 * SUBS,)),
            dma((7,)), dma((7,)), dma((3,)), dma((3,)), dma((7,)), dma((7,)), dma((14,)), dma((14,)),
            dma((72,)), dma((72,)),
        ],
        compiler_params=pltpu.CompilerParams(
            collective_id=0, has_side_effects=True, vmem_limit_bytes=60 << 20
        ),
        name="state_and_gather",
    )(q, k, v, w, cw)


def heads_of(j):
    features = [
        feature_of(p) for p in range(LANES * j, LANES * (j + 1)) if p % BLKP < BLK
    ]
    first, last = min(features) // HD, max(features) // HD
    lo = HD * first // LANES * LANES
    hi = min(-(-HD * (last + 1) // LANES) * LANES, D)
    return first, last, lo, hi


def shards(queries, keys, values, conv_weight, w_out):
    q, k, v = (a.reshape(TOK, D) for a in (queries, keys, values))
    out, _ = gather(q, k, v, w_out, conv_weight)
    return out[:, :D].reshape(1, ROWS, COLS, D)


def solution(mesh):
    placed = P("tm", "space", None, None)
    return jax.shard_map(
        shards,
        mesh=mesh,
        in_specs=(placed, placed, placed, P(), P("tm", "space")),
        out_specs=placed,
        check_vma=False,
    )
```

```python
import functools

import jax
import jax.numpy as jnp
from jax import lax
from jax.experimental import pallas as pl
from jax.experimental.pallas import tpu as pltpu
from jax.sharding import PartitionSpec as P

HEADS = 20
HD = 112
D = HEADS * HD
ROWS, COLS = 8, 80
TOK = ROWS * COLS
LANES = 128
TILES = 18
DP = TILES * LANES
BLK, BLKP = 70, 72
UNITS = 7
NZ = 8
EPS = 1e-06
FIRST = 1536
SUBS = 4
PART = 16 // SUBS
MESH = pl.DeviceIdType.MESH
F32, BF16 = jnp.float32, jnp.bfloat16


def feature_of(pos):
    return BLK * (pos // BLKP) + min(pos % BLKP, BLK - 1)


def spread_window(j):
    lo = feature_of(LANES * j) // LANES
    lo = min(lo, TILES - 2)
    return lo, LANES * lo, min(LANES * (lo + 2), D)


def spread_matrix(j, start, stop):
    shape = (stop - start, LANES)
    pos = LANES * j + lax.broadcasted_iota(jnp.int32, shape, 1)
    block = lax.shift_right_logical(pos * 14564, 20)
    inside = pos - BLKP * block
    feature = BLK * block + inside
    row = start + lax.broadcasted_iota(jnp.int32, shape, 0)
    return jnp.where((row == feature) & (inside < BLK), 1.0, 0.0).astype(BF16)


def dot(a, b):
    return jnp.dot(a, b, preferred_element_type=F32)


def add_mod(a, b, n):
    return lax.rem(a + b + 2 * n, n)


def gather_kernel(
    q_hbm, k_hbm, v_hbm, w_hbm, cw_hbm, out_hbm, wg_hbm,
    cw_ref, kn, vn, kt, vp, cwp, conv, z_ref, fwd, bwd, own, scan, pre, xs, back, s_own, wa, wown,
    s_all, sn, band, spreads, picks, qv, mix, wv, out_v,
    local_sem, halo_send, halo_recv, wa_send, wa_recv, rs_send, rs_recv, sc_send, sc_recv,
    xs_send, xs_recv, bk_send, bk_recv, ag_send, ag_recv, wg_send, wg_recv,
):
    tm, z = lax.axis_index("tm"), lax.axis_index("space")
    core, y, x = lax.rem(tm, 2), lax.rem(lax.div(tm, 2), 4), lax.div(tm, 8)
    member = lax.rem(tm, 8)
    dr = 1 - 2 * core

    def at(xx, yy, cc):
        return 8 * xx + 2 * yy + cc

    def along_a(k):
        other = add_mod(jnp.where(core == 0, x, y), k, 4)
        return jnp.where(core == 0, at(other, y, core), at(x, other, core))

    def along(ka, kb):
        px = add_mod(x, jnp.where(core == 0, ka, kb), 4)
        py = add_mod(y, jnp.where(core == 0, kb, ka), 4)
        return at(px, py, core)

    partner = at(x, y, 1 - core)
    everything = []

    def remote(src, dst, send, recv, to_tm, to_z):
        return pltpu.make_async_remote_copy(
            src_ref=src, dst_ref=dst, send_sem=send, recv_sem=recv,
            device_id={"tm": to_tm, "space": to_z}, device_id_type=MESH,
        )

    def start(copy):
        copy.start()
        everything.append(copy)
        return copy

    barrier = pltpu.get_barrier_semaphore()
    friends = [(tm, add_mod(z, o, NZ)) for o in range(1, NZ)]
    friends += [(8 * x + add_mod(member, o, 8), z) for o in range(1, 8)]
    friends += [(add_mod(tm, 8 * o, 32), z) for o in range(1, 4)]
    for to_tm, to_z in friends:
        pl.semaphore_signal(barrier, inc=1, device_id={"tm": to_tm, "space": to_z}, device_id_type=MESH)
    loads = [
        pltpu.make_async_copy(k_hbm, kn, local_sem.at[0]),
        pltpu.make_async_copy(v_hbm, vn.at[pl.ds(COLS, TOK)], local_sem.at[1]),
    ]
    load_cw = pltpu.make_async_copy(cw_hbm, cw_ref, local_sem.at[6])
    for copy in loads:
        copy.start()
    pl.semaphore_wait(barrier, len(friends))

    wa_mine = pltpu.make_async_copy(w_hbm, wa.at[z], local_sem.at[2])
    wa_mine.start()
    load_cw.start()
    for n, o in enumerate((1, -1, 2, -2)):
        start(remote(w_hbm, wa.at[z], wa_send.at[n], wa_recv.at[n], tm, add_mod(z, o, NZ)))
    halo = [
        remote(v_hbm.at[pl.ds(0, COLS)], vn.at[pl.ds(COLS + TOK, COLS)], halo_send.at[0], halo_recv.at[0], tm, add_mod(z, -1, NZ)),
        remote(v_hbm.at[pl.ds(TOK - COLS, COLS)], vn.at[pl.ds(0, COLS)], halo_send.at[1], halo_recv.at[1], tm, add_mod(z, 1, NZ)),
    ]

    def partial_state():
        loads[0].wait()
        for i in range(TILES):
            lo, hi = LANES * i, min(LANES * (i + 1), D)
            kt[lo:hi, :] = jnp.maximum(kn[:, lo:hi], 0).T
        loads[1].wait()
        ones = jnp.ones((TOK, LANES), BF16)
        lane = lax.broadcasted_iota(jnp.int32, (HD, LANES), 1)
        sums = jnp.zeros((HD, LANES), F32)
        for j in range(TILES):
            lo, hi = LANES * j, min(LANES * (j + 1), D)
            tile = vn[COLS : COLS + TOK, lo:hi]
            if hi - lo < LANES:
                eye = lax.broadcasted_iota(jnp.int32, (hi - lo, LANES), 0) == lax.broadcasted_iota(jnp.int32, (hi - lo, LANES), 1)
                tile = dot(tile, jnp.where(eye, 1.0, 0.0).astype(BF16)).astype(BF16)
            first, last = lo // HD, (hi - 1) // HD
            g = dot(kt[HD * first : HD * (last + 1), :], jnp.concatenate([tile, ones], axis=1))
            part = g[:HD, :LANES]
            for h in range(first, last + 1):
                rows = g[HD * (h - first) : HD * (h - first + 1)]
                part = jnp.where(lane < HD * h - lo, part, rows[:, :LANES])
                sums = jnp.where(lane == D - LANES * (TILES - 1) + h, rows[:, LANES:], sums)
            if j == TILES - 1:
                part = jnp.where(lane < D - lo, part, sums)
            for r in range(UNITS):
                z_ref[UNITS * j + r] = part[16 * r : 16 * (r + 1)]
        z_ref[UNITS * TILES] = jnp.zeros((16, LANES), F32)
        z_ref[UNITS * TILES + 1] = jnp.zeros((16, LANES), F32)

    def ring(forward, s, u):
        hops = 4 if forward else 3
        way = dr if forward else -dr
        slots = fwd if forward else bwd
        chunk = add_mod(z, way * (hops - s), NZ)
        place = pl.ds(PART * u, PART)
        sem = (0 if forward else 4 * SUBS) + SUBS * s + u
        if s == 0:
            src = z_ref.at[pl.ds(16 * chunk + PART * u, PART)]
        else:
            everything_rs[(forward, s - 1, u)].wait_recv()
            slots[s - 1, place] += z_ref[pl.ds(16 * chunk + PART * u, PART)]
            src = slots.at[s - 1, place]
        copy = remote(src, slots.at[s, place], rs_send.at[sem], rs_recv.at[sem], tm, add_mod(z, way, NZ))
        copy.start()
        everything_rs[(forward, s, u)] = copy

    everything_rs = {}

    def ring_step(s):
        for u in range(SUBS):
            ring(True, s, u)
            if s < 3:
                ring(False, s, u)

    def ring_end():
        for u in range(SUBS):
            everything_rs[(True, 3, u)].wait_recv()
            everything_rs[(False, 2, u)].wait_recv()
            place = pl.ds(PART * u, PART)
            own[place] = z_ref[pl.ds(16 * z + PART * u, PART)] + fwd[3, place] + bwd[2, place]

    def scan_send():
        for o in range(1, 8):
            other = add_mod(member, o, 8)
            start(remote(own.at[pl.ds(2 * other, 2)], scan.at[member], sc_send.at[o - 1], sc_recv.at[o - 1], 8 * x + other, z))
        scan[member] = own[pl.ds(2 * member, 2)]

    def scan_group():
        for o in range(1, 8):
            remote(own.at[pl.ds(0, 2)], scan.at[0], sc_send.at[o - 1], sc_recv.at[o - 1], tm, z).wait_recv()
        total = jnp.zeros((2, 16, LANES), F32)
        for m in range(8):
            total = total + scan[m]
            pre[m] = total
        for o in range(1, 4):
            start(remote(pre.at[7], xs.at[x], xs_send.at[o - 1], xs_recv.at[o - 1], add_mod(tm, 8 * o, 32), z))
        xs[x] = total

    def scan_back():
        for o in range(1, 4):
            remote(pre.at[7], xs.at[0], xs_send.at[o - 1], xs_recv.at[o - 1], tm, z).wait_recv()
        before = jnp.zeros((2, 16, LANES), F32)
        for k in range(4):
            before = before + jnp.where(k < x, xs[k], 0.0)
        for m in range(8):
            back[m] = (before + pre[m]).astype(BF16)
        for o in range(1, 8):
            other = add_mod(member, o, 8)
            start(remote(back.at[other], s_own.at[pl.ds(2 * member, 2)], bk_send.at[o - 1], bk_recv.at[o - 1], 8 * x + other, z))
        s_own[pl.ds(2 * member, 2)] = back[member]

    def share_state():
        for o in range(1, 8):
            remote(back.at[0], s_own.at[pl.ds(0, 2)], bk_send.at[o - 1], bk_recv.at[o - 1], tm, z).wait_recv()
        for h in range(2):
            for o in (1, -1, 2, -2):
                state_send(share_number[o] + h, s_own.at[pl.ds(8 * h, 8)], part_of(0, h), o)
        copy = pltpu.make_async_copy(s_own, s_all.at[pl.ds(16 * z, 16)], local_sem.at[3])
        copy.start()
        return copy

    share_number = {1: 0, -1: 2, 2: 4, -2: 6}

    def part_of(o, h):
        return s_all.at[pl.ds(16 * add_mod(z, o, NZ) + 8 * h, 8)]

    def state_send(n, src, dst, o):
        start(remote(src, dst, ag_send.at[n], ag_recv.at[n], tm, add_mod(z, o, NZ)))

    def state_wait(n, ref):
        remote(ref, ref, ag_send.at[n], ag_recv.at[n], tm, z).wait_recv()

    def pass_on_state():
        for h in range(2):
            state_wait(4 + h, part_of(-2, h))
            state_send(8 + h, part_of(-2, h), part_of(-2, h), 1)
            if h == 0:
                state_send(12, part_of(-2, 0), part_of(-2, 0), 2)
            state_wait(6 + h, part_of(2, h))
            state_send(10 + h, part_of(2, h), part_of(2, h), -1)
            if h == 1:
                state_send(13, part_of(2, 1), part_of(2, 1), -2)

    def state_end():
        for n, (o, h) in {0: (-1, 0), 1: (-1, 1), 2: (1, 0), 3: (1, 1)}.items():
            state_wait(n, part_of(o, h))
        for n, (o, h) in {8: (-3, 0), 9: (-3, 1), 10: (3, 0), 11: (3, 1), 12: (4, 0), 13: (4, 1)}.items():
            state_wait(n, part_of(o, h))

    def rows_of(owner, half=None, p=0):
        lo, n = (0, BLKP) if half is None else ((0, 40) if half == 0 else (40, 32))
        return wg_hbm.at[pl.ds(pl.multiple_of(BLKP * owner + lo, 8), n), columns(p)]

    def columns(p):
        return pl.ds(0, FIRST) if p == 0 else pl.ds(FIRST, DP - FIRST)

    def w_send(n, src, dst, to_tm, p):
        start(remote(src, dst, wg_send.at[36 * p + n], wg_recv.at[36 * p + n], to_tm, z))

    def w_wait(n, ref, p):
        remote(ref, ref, wg_send.at[36 * p + n], wg_recv.at[36 * p + n], tm, z).wait_recv()

    deltas = (0, -1, 1, 2)

    def w_out_b(g, p):
        owner = along(deltas[g], 0)
        ref = rows_of(owner, p=p) if g else wown.at[:, columns(p)]
        to = rows_of(owner, p=p)
        w_send(4 + 4 * g, ref, to, along(0, 1), p)
        w_send(5 + 4 * g, ref, to, along(0, -1), p)
        w_send(20 + 4 * g, ref, to, partner, p)

    def wa_wait(n):
        remote(w_hbm, wa.at[0], wa_send.at[n], wa_recv.at[n], tm, z).wait_recv()

    def wa_pass_on():
        wa_wait(2)
        wa_wait(3)
        below, above = add_mod(z, -2, NZ), add_mod(z, 2, NZ)
        far = add_mod(z, -2 * dr, NZ)
        for n, slot, to in ((4, below, add_mod(z, 1, NZ)), (5, above, add_mod(z, -1, NZ)), (6, far, add_mod(z, 2 * dr, NZ))):
            start(remote(wa.at[slot], wa.at[slot], wa_send.at[n], wa_recv.at[n], tm, to))

    def w_assemble():
        wa_mine.wait()
        for n in (0, 1, 4, 5, 6):
            wa_wait(n)
        wown[...] = jnp.zeros((BLKP, DP), BF16)
        width = D // NZ
        for j in range(TILES):
            lo, hi = LANES * j, min(LANES * (j + 1), D)
            acc = jnp.zeros((BLK, LANES), F32)
            for b in range(lo // width, (hi - 1) // width + 1):
                row = width * b + lax.broadcasted_iota(jnp.int32, (width, LANES), 0)
                col = lo + lax.broadcasted_iota(jnp.int32, (width, LANES), 1)
                acc = acc + dot(wa[b], jnp.where(row == col, 1.0, 0.0).astype(BF16))
            wown[0:BLK, lo : lo + LANES] = acc.astype(BF16)
        mine = [
            pltpu.make_async_copy(wown.at[:, columns(p)], rows_of(tm, p=p), local_sem.at[(4, 10)[p]])
            for p in range(2)
        ]
        for copy in mine:
            copy.start()
        return mine

    def w_out_a(p):
        for n, k in enumerate((1, -1)):
            w_send(n, wown.at[:, columns(p)], rows_of(tm, p=p), along(k, 0), p)

    def w_pass_full(p):
        low, high = along(-1, 0), along(1, 0)
        w_wait(0, rows_of(low, p=p), p)
        w_wait(1, rows_of(high, p=p), p)
        w_send(2, rows_of(low, 0, p), rows_of(low, 0, p), high, p)
        w_send(3, rows_of(high, 1, p), rows_of(high, 1, p), low, p)

    def w_wait_half(p):
        w_wait(2, rows_of(along(2, 0), 0, p), p)
        w_wait(3, rows_of(along(2, 0), 1, p), p)

    def w_b_full(g, p):
        low, high = along(deltas[g], -1), along(deltas[g], 1)
        w_wait(4 + 4 * g, rows_of(low, p=p), p)
        w_send(6 + 4 * g, rows_of(low, 0, p), rows_of(low, 0, p), along(0, 1), p)
        w_wait(5 + 4 * g, rows_of(high, p=p), p)
        w_send(7 + 4 * g, rows_of(high, 1, p), rows_of(high, 1, p), along(0, -1), p)
        w_send(21 + 4 * g, rows_of(low, p=p), rows_of(low, p=p), partner, p)
        w_send(22 + 4 * g, rows_of(high, p=p), rows_of(high, p=p), partner, p)

    def w_b_half(g, p):
        far = along(deltas[g], 2)
        w_wait(6 + 4 * g, rows_of(far, 0, p), p)
        w_wait(7 + 4 * g, rows_of(far, 1, p), p)
        w_send(23 + 4 * g, rows_of(far, p=p), rows_of(far, p=p), partner, p)

    def w_end(p):
        for n in range(20, 36):
            w_wait(n, rows_of(0, p=p), p)

    def conv_prepare():
        load_cw.wait()
        for j in range(TILES):
            _, lo, hi = spread_window(j)
            spread = spreads[j, : hi - lo, :]
            place = slice(LANES * j, LANES * (j + 1))
            vp[COLS : COLS + TOK, place] = dot(vn[COLS : COLS + TOK, lo:hi], spread).astype(BF16)
            for a in range(3):
                rest = cw_ref[a, :, lo:hi]
                total = jnp.zeros((3, LANES), F32)
                for _ in range(3):
                    piece = rest.astype(BF16)
                    total = total + dot(piece, spread)
                    rest = rest - piece.astype(F32)
                cwp[a, 0:3, place] = total

    def conv_rims():
        for copy in halo:
            copy.wait_recv()
        for n, start_row in enumerate((0, COLS + TOK)):
            there = jnp.where(z == (0, NZ - 1)[n], 0.0, 1.0)
            for j in range(TILES):
                _, lo, hi = spread_window(j)
                rim = dot(vn[start_row : start_row + COLS, lo:hi], spreads[j, : hi - lo, :])
                vp[start_row : start_row + COLS, LANES * j : LANES * (j + 1)] = (rim * there).astype(BF16)

    def conv_rows(first, last):
        row = lax.broadcasted_iota(jnp.int32, (COLS, LANES), 0)

        @pl.loop(first, last)
        def _(r):
            base = pl.multiple_of(COLS * r, 16)
            for j in range(TILES):
                place = slice(LANES * j, LANES * (j + 1))
                lines = [vp[pl.ds(base + COLS * a, COLS), place].astype(F32) for a in range(3)]
                sums = []
                for b in range(3):
                    sums.append(sum(lines[a] * cwp[a, b : b + 1, place] for a in range(3)))
                left = jnp.where(row == 0, 0.0, pltpu.roll(sums[0], 1, 0))
                right = jnp.where(row == COLS - 1, 0.0, pltpu.roll(sums[2], COLS - 1, 0))
                conv[pl.ds(base, COLS), place] = sums[1] + left + right

    def make_masks():
        base = D - LANES * (TILES - 1)
        pos = lax.broadcasted_iota(jnp.int32, (LANES, LANES), 1)
        row = lax.broadcasted_iota(jnp.int32, (LANES, LANES), 0)
        for j in range(TILES):
            _, lo, _ = spread_window(j)
            spreads[j] = spread_matrix(j, lo, lo + 2 * LANES)
        n = 0
        for j in range(TILES):
            for h, from_lane, to_lane in head_lanes(j):
                at = (pos >= from_lane) & (pos < to_lane) & (row == base + h)
                picks[n] = jnp.where(at, 1.0, 0.0).astype(BF16)
                n += 1

    def clear_bands():
        for j in range(TILES):
            band[j] = jnp.zeros(band.shape[1:], BF16)

    def make_bands():
        for j in range(TILES):
            for r in range(UNITS):
                sn[16 * r : 16 * (r + 1), LANES * j : LANES * (j + 1)] = s_all[UNITS * j + r]
        sums = sn[:, LANES * (TILES - 1) :]
        lane = lax.broadcasted_iota(jnp.int32, (1, LANES), 1)
        n = 0
        for j in range(TILES):
            _, _, lo, _ = heads_of(j)
            _, w_lo, _ = spread_window(j)
            state = dot(sn[:, w_lo : w_lo + 2 * LANES], spreads[j]).astype(BF16)
            for h, from_lane, to_lane in head_lanes(j):
                keep = jnp.where((lane >= from_lane) & (lane < to_lane), 1.0, 0.0).astype(BF16)
                at = slice(HD * h - lo, HD * (h + 1) - lo)
                band[j, at, :LANES] = state * keep
                band[j, at, LANES:] = dot(sums, picks[n]).astype(BF16)
                n += 1

    def attend(tiles):
        for j in tiles:
            _, _, lo, hi = heads_of(j)
            place = slice(LANES * j, LANES * (j + 1))
            both = dot(jnp.maximum(qv[:, lo:hi], 0), band[j, : hi - lo, :])
            mix[:, place] = (both[:, :LANES] / (both[:, LANES:] + EPS) + conv[:, place]).astype(BF16)

    def project(lo, hi):
        @pl.loop(lo, hi)
        def _(n):
            at = pl.ds(pl.multiple_of(256 * n, 256), 256)
            out_v[:, at] = dot(mix[...], wv[:, at]).astype(BF16)

    load_q = pltpu.make_async_copy(q_hbm, qv, local_sem.at[7])
    load_w = [
        pltpu.make_async_copy(wg_hbm.at[:, columns(p)], wv.at[:, columns(p)], local_sem.at[(8, 5)[p]])
        for p in range(2)
    ]
    save_out = [
        pltpu.make_async_copy(out_v.at[:, columns(p)], out_hbm.at[:, columns(p)], local_sem.at[(9, 11)[p]])
        for p in range(2)
    ]

    partial_state()
    ring_step(0)
    load_q.start()
    make_masks()
    ring_step(1)
    wa_pass_on()
    conv_prepare()
    ring_step(2)
    mine = w_assemble()
    w_out_a(0)
    w_out_b(0, 0)
    w_out_a(1)
    ring_step(3)
    for copy in halo:
        start(copy)
    conv_rows(1, 4)
    ring_end()
    scan_send()
    w_pass_full(0)
    w_out_b(1, 0)
    w_b_full(0, 0)
    clear_bands()
    conv_rows(4, 6)
    scan_group()
    w_out_b(2, 0)
    w_pass_full(1)
    conv_rows(6, 7)
    scan_back()
    w_wait_half(0)
    w_out_b(3, 0)
    w_out_b(0, 1)
    state_mine = share_state()
    w_b_full(1, 0)
    w_b_half(0, 0)
    w_out_b(1, 1)
    conv_rims()
    conv_rows(0, 1)
    conv_rows(7, 8)
    pass_on_state()
    w_b_full(2, 0)
    w_b_full(3, 0)
    w_b_full(0, 1)
    w_out_b(2, 1)
    w_wait_half(1)
    w_out_b(3, 1)
    state_end()
    state_mine.wait()
    w_b_half(1, 0)
    w_b_half(2, 0)
    w_b_full(1, 1)
    make_bands()
    w_b_half(3, 0)
    w_b_full(2, 1)
    load_q.wait()
    attend(range(0, 5))
    for copy in mine:
        copy.wait()
    w_end(0)
    load_w[0].start()
    w_b_full(3, 1)
    attend(range(5, TILES))
    w_b_half(0, 1)
    w_b_half(1, 1)
    load_w[0].wait()
    project(0, 1)
    w_b_half(2, 1)
    w_b_half(3, 1)
    project(1, 3)
    w_end(1)
    load_w[1].start()
    project(3, 6)
    save_out[0].start()
    load_w[1].wait()
    project(6, 9)
    save_out[1].start()
    for copy in everything + list(everything_rs.values()):
        copy.wait_send()
    for copy in save_out:
        copy.wait()


def head_lanes(j):
    heads = {}
    for lane in range(LANES):
        heads.setdefault(feature_of(LANES * j + lane) // HD, []).append(lane)
    return [(h, min(lanes), max(lanes) + 1) for h, lanes in sorted(heads.items())]


def gather(q, k, v, w, cw):
    dma = pltpu.SemaphoreType.DMA
    any_space = pl.BlockSpec(memory_space=pl.ANY)
    return pl.pallas_call(
        gather_kernel,
        out_shape=(
            jax.ShapeDtypeStruct((TOK, DP), BF16),
            jax.ShapeDtypeStruct((32 * BLKP, DP), BF16),
        ),
        in_specs=[pl.BlockSpec(memory_space=pltpu.HBM)] * 5,
        out_specs=(any_space,) * 2,
        scratch_shapes=[
            pltpu.VMEM((3, 3, D), F32),
            pltpu.VMEM((TOK, D), BF16),
            pltpu.VMEM((TOK + 2 * COLS, D), BF16),
            pltpu.VMEM((D, TOK), BF16),
            pltpu.VMEM((TOK + 2 * COLS, DP), BF16),
            pltpu.VMEM((3, 8, DP), F32),
            pltpu.VMEM((TOK, DP), F32),
            pltpu.VMEM((16 * NZ, 16, LANES), F32),
            pltpu.VMEM((4, 16, 16, LANES), F32),
            pltpu.VMEM((3, 16, 16, LANES), F32),
            pltpu.VMEM((16, 16, LANES), F32),
            pltpu.VMEM((8, 2, 16, LANES), F32),
            pltpu.VMEM((8, 2, 16, LANES), F32),
            pltpu.VMEM((4, 2, 16, LANES), F32),
            pltpu.VMEM((8, 2, 16, LANES), BF16),
            pltpu.VMEM((16, 16, LANES), BF16),
            pltpu.VMEM((NZ, BLK, D // NZ), BF16),
            pltpu.VMEM((BLKP, DP), BF16),
            pltpu.VMEM((16 * NZ, 16, LANES), BF16),
            pltpu.VMEM((HD, DP), BF16),
            pltpu.VMEM((TILES, 512, 256), BF16),
            pltpu.VMEM((TILES, 256, LANES), BF16),
            pltpu.VMEM((sum(len(head_lanes(j)) for j in range(TILES)), LANES, LANES), BF16),
            pltpu.VMEM((TOK, D), BF16),
            pltpu.VMEM((TOK, DP), BF16),
            pltpu.VMEM((32 * BLKP, DP), BF16),
            pltpu.VMEM((TOK, DP), BF16),
            dma((12,)), dma((2,)), dma((2,)), dma((7,)), dma((7,)), dma((7 * SUBS,)), dma((7 * SUBS,)),
            dma((7,)), dma((7,)), dma((3,)), dma((3,)), dma((7,)), dma((7,)), dma((14,)), dma((14,)),
            dma((72,)), dma((72,)),
        ],
        compiler_params=pltpu.CompilerParams(
            collective_id=0, has_side_effects=True, vmem_limit_bytes=60 << 20
        ),
        name="state_and_gather",
    )(q, k, v, w, cw)


def heads_of(j):
    features = [
        feature_of(p) for p in range(LANES * j, LANES * (j + 1)) if p % BLKP < BLK
    ]
    first, last = min(features) // HD, max(features) // HD
    lo = HD * first // LANES * LANES
    hi = min(-(-HD * (last + 1) // LANES) * LANES, D)
    return first, last, lo, hi


def shards(queries, keys, values, conv_weight, w_out):
    q, k, v = (a.reshape(TOK, D) for a in (queries, keys, values))
    out, _ = gather(q, k, v, w_out, conv_weight)
    return out[:, :D].reshape(1, ROWS, COLS, D)


def solution(mesh):
    placed = P("tm", "space", None, None)
    return jax.shard_map(
        shards,
        mesh=mesh,
        in_specs=(placed, placed, placed, P(), P("tm", "space")),
        out_specs=placed,
        check_vma=False,
    )
```
